32 devices in a mesh: dp: 8 (over z, x), seq: 4 (over y, core).
Axes of the slice: x: 2, y: 2, z: 4, core: 2. Of those that a mesh axis runs over, the one named last changes fastest.
Arguments:
- spatial_qkv: bfloat16 [8, 3, 4, 128, 1152], P('dp', None, 'seq'), may hold values from -24 to 24
- temporal_qkv: bfloat16 [8, 3, 4, 128, 1152], P('dp', None, 'seq'), may hold values from -24 to 24
- cotangent: bfloat16 [8, 4, 128, 1152], P('dp', 'seq'), may hold values from -6 to 6
- spatial_gate: float32 [8, 1152], P('dp'), may hold values from -4 to 4
- temporal_gate: float32 [8, 1152], P('dp'), may hold values from -4 to 4
- temporal_proj: bfloat16 [1152, 1152], replicated, may hold values from -0.1875 to 0.1875
- live_counts: int32 [8, 2], P('dp'), may hold values from 2 to 128, as said below
Outputs:
- temporal_qkv_grad: bfloat16 [8, 3, 4, 128, 1152], P('dp', None, 'seq')
- spatial_proj_grad: float32 [1152, 1152], P('seq', 'dp')
- temporal_proj_grad: float32 [1152, 1152], P('seq', 'dp')
The draws below stay inside these ranges and needn't reach their ends.
Inputs may be any that keep to these rules, and one draw needn't show every extreme that they name: live_counts[g, 0] counts a clip's live frames, at most 4; live_counts[g, 1] counts the live positions of each of its frames, at most 128; in every draw some clip has all 4 frames and all 128 positions live.
All inputs are finite; a program needn't handle non-finite values.
Results may differ from the reference program's by a relative error of at most 0.015.
Values may be sent and summed in bfloat16 or wider, within the bound.
A program may use at most 64 MiB of HBM per device.

```python
import jax
import jax.numpy as jnp
from jax import lax

D = 1152
HEADS = 16
FR_DEV = 1
POS = 128
HD = 72
FRAMES = 4
GROUPS = 8
N_SEQ = 4


def make_attention_inputs(base_key):
    first_key = jax.random.fold_in(base_key, 0)
    drawn = jax.random.truncated_normal(first_key, -6.0, 6.0, (GROUPS, 3, FRAMES, POS, D), jnp.float32)
    return drawn.astype(jnp.bfloat16)


def draw_spatial_qkv(key, part):
    return make_attention_inputs(jax.random.fold_in(key, 11))


def draw_temporal_qkv(key, part):
    return make_attention_inputs(jax.random.fold_in(key, 12))


def draw_live_counts(key, part):
    first_key, second_key, third_key = jax.random.split(jax.random.fold_in(key, 13), 3)
    frame_counts = jax.random.randint(first_key, (GROUPS,), max(2, FRAMES // 4), FRAMES + 1)
    position_counts = jax.random.randint(second_key, (GROUPS,), max(2, POS // 4), POS + 1)
    full_group = jax.random.randint(third_key, (), 0, GROUPS)
    group_ids = jnp.arange(GROUPS)
    frame_counts = jnp.where(group_ids == full_group, FRAMES, frame_counts)
    position_counts = jnp.where(group_ids == full_group, POS, position_counts)
    return jnp.stack([frame_counts, position_counts], axis=1).astype(jnp.int32)


def level_of(stream_key, dims, pieces, low, high):
    factor_of = 1.0
    for dim, blocks in pieces:
        steps = jax.random.uniform(jax.random.fold_in(jax.random.fold_in(stream_key, 6), dim), (blocks,), jnp.float32, low / len(pieces), high / len(pieces))
        factor_of = factor_of * jnp.repeat(jnp.exp(steps), dims[dim] // blocks).reshape((-1,) + (1,) * (len(dims) - 1 - dim))
    return factor_of


def normal_values(own_key, shape, width, most, cuts=(), kind=jnp.bfloat16):
    gain = level_of(own_key, shape, cuts, -0.22, 0.18) if cuts else 1.0
    array = jax.random.normal(own_key, shape, jnp.float32) * width * gain
    return jnp.minimum(jnp.maximum(array, -most), most).astype(kind)


def setup_inputs(seed: int = 0) -> dict:
    splits = jax.random.split(jax.random.key(seed), 8)
    spatial_qkv = draw_spatial_qkv(jax.random.fold_in(splits[7], 71), 0)
    temporal_qkv = draw_temporal_qkv(jax.random.fold_in(splits[7], 71), 0)
    cotangent = normal_values(splits[2], (GROUPS, FRAMES, POS, D), 1.0, 6.0, ((0, 8), (1, 4)))
    spatial_gate = normal_values(splits[3], (GROUPS, D), 1.0, 4.0, ((0, 8),), jnp.float32)
    temporal_gate = normal_values(splits[4], (GROUPS, D), 1.0, 4.0, ((0, 8),), jnp.float32)
    temporal_proj = normal_values(splits[5], (D, D), D ** -0.5, 0.1875)
    live_counts = draw_live_counts(jax.random.fold_in(splits[7], 71), 0)
    return {"spatial_qkv": spatial_qkv, "temporal_qkv": temporal_qkv, "cotangent": cotangent, "spatial_gate": spatial_gate, "temporal_gate": temporal_gate, "temporal_proj": temporal_proj, "live_counts": live_counts}


def attend(queries, key_block, value_block, key_keep, score_form, mix_form):
    head_split = queries.shape[:-1] + (HEADS, HD)
    q_heads = queries.astype(jnp.float32).reshape(head_split)
    k_heads = key_block.astype(jnp.float32).reshape(head_split)
    v_heads = value_block.astype(jnp.float32).reshape(head_split)
    scores = jnp.einsum(score_form, q_heads, k_heads) * HD ** (-0.5)
    scores = jnp.where(key_keep[:, None, None, :], scores, -1e+30)
    shifted = scores - lax.optimization_barrier(jnp.max(scores, axis=-1, keepdims=True))
    expo = jnp.exp(shifted)
    attention_weights = expo / lax.optimization_barrier(jnp.sum(expo, axis=-1, keepdims=True))
    rounded = lax.optimization_barrier(attention_weights.astype(jnp.bfloat16)).astype(jnp.float32)
    mixed = jnp.einsum(mix_form, rounded, v_heads)
    return mixed.reshape(queries.shape)

def block_parts(outputs, errors):
    left = outputs.reshape(N_SEQ, FR_DEV * POS, D).astype(jnp.float32)
    right = errors.reshape(N_SEQ, FR_DEV * POS, D).astype(jnp.float32)
    parts = jnp.einsum('btr,btc->brc', left, right)
    parts = lax.optimization_barrier(parts.astype(jnp.bfloat16)).astype(jnp.float32)
    return lax.optimization_barrier(jnp.sum(parts, axis=0))

def reference(spatial_qkv, temporal_qkv, cotangent, spatial_gate, temporal_gate, temporal_proj, live_counts):

    def one_group(accumulated, group_items):
        s_qkv, t_qkv, incoming, s_gate, t_gate, counts = group_items
        frame_ids = jnp.arange(FRAMES, dtype=jnp.int32)
        position_ids = jnp.arange(POS, dtype=jnp.int32)
        token_mask = ((frame_ids[:, None] < counts[0]) & (position_ids[None, :] < counts[1])).astype(jnp.float32)
        flowing = token_mask[:, :, None] * incoming.astype(jnp.float32)
        spatial_error = (flowing * s_gate).astype(jnp.bfloat16)
        temporal_error = (flowing * t_gate).astype(jnp.bfloat16)
        temporal_back = jnp.dot(temporal_error.reshape(FRAMES * POS, D), temporal_proj.T, preferred_element_type=jnp.float32).astype(jnp.bfloat16).reshape(FRAMES, POS, D)
        spatial_keep = jnp.broadcast_to(position_ids[None, :] < counts[1], (FRAMES, POS))
        spatial_out = attend(s_qkv[0], s_qkv[1], s_qkv[2], spatial_keep, 'bqhd,bkhd->bhqk', 'bhqk,bkhd->bqhd').astype(jnp.bfloat16)
        temporal_keep = jnp.broadcast_to(frame_ids[None, :] < counts[0], (POS, FRAMES))

        def temporal_attend(queries, key_block, value_block):
            return attend(queries, key_block, value_block, temporal_keep, 'qbhd,kbhd->bhqk', 'bhqk,kbhd->qbhd')
        temporal_result, pullback = jax.vjp(temporal_attend, t_qkv[0], t_qkv[1], t_qkv[2])
        temporal_out = temporal_result.astype(jnp.bfloat16)
        input_grads = jnp.stack(pullback(temporal_back.astype(jnp.float32)))
        spatial_sum = accumulated[0] + block_parts(spatial_out, spatial_error)
        temporal_sum = accumulated[1] + block_parts(temporal_out, temporal_error)
        return ((spatial_sum, temporal_sum), input_grads)
    start = (jnp.zeros((D, D), jnp.float32), jnp.zeros((D, D), jnp.float32))
    sums, all_grads = lax.scan(one_group, start, (spatial_qkv, temporal_qkv, cotangent, spatial_gate, temporal_gate, live_counts))
    return (all_grads, sums[0], sums[1])
```

```python
import functools

import jax
import jax.numpy as jnp
from jax import lax
from jax.experimental import pallas as pl
from jax.experimental.pallas import tpu as pltpu
from jax.sharding import PartitionSpec as P

HEADS = 16
HD = 72
MESH = pl.DeviceIdType.MESH
F32 = jnp.float32
BF16 = jnp.bfloat16


def attend(queries, key_block, value_block, key_keep, score_form, mix_form):
    head_split = queries.shape[:-1] + (HEADS, HD)
    q_heads = queries.reshape(head_split)
    k_heads = key_block.reshape(head_split)
    v_heads = value_block.reshape(head_split)
    scores = jnp.einsum(score_form, q_heads, k_heads, preferred_element_type=jnp.float32) * HD ** (
        -0.5
    )
    scores = jnp.where(key_keep[:, None, None, :], scores, -1e30)
    shifted = scores - jnp.max(scores, axis=-1, keepdims=True)
    expo = jnp.exp(shifted)
    attention_weights = (expo / jnp.sum(expo, axis=-1, keepdims=True)).astype(jnp.bfloat16)
    mixed = jnp.einsum(mix_form, attention_weights, v_heads, preferred_element_type=jnp.float32)
    return mixed.reshape(queries.shape)


def body(
    spatial_qkv, temporal_qkv, cotangent, spatial_gate, temporal_gate, temporal_proj, live_counts
):
    spatial = spatial_qkv[0]
    temporal = temporal_qkv[0]
    incoming = cotangent[0]
    frame_count, position_count, width = incoming.shape
    group_size = lax.axis_size("seq")
    member = lax.axis_index("seq")
    live_frames = live_counts[0, 0]
    live_positions = live_counts[0, 1]
    frame_ids = member * frame_count + jnp.arange(frame_count, dtype=jnp.int32)
    position_ids = jnp.arange(position_count, dtype=jnp.int32)
    token_mask = (
        (frame_ids[:, None] < live_frames) & (position_ids[None, :] < live_positions)
    ).astype(jnp.float32)
    flowing = token_mask[:, :, None] * incoming.astype(jnp.float32)
    temporal_error = (flowing * temporal_gate[0]).astype(jnp.bfloat16)
    temporal_back = lax.dot_general(
        temporal_error, temporal_proj, (((2,), (1,)), ((), ())), preferred_element_type=jnp.float32
    ).astype(jnp.bfloat16)
    stacked = jnp.concatenate([temporal, temporal_back[None]], axis=0)
    exchanged = lax.all_to_all(stacked, "seq", split_axis=2, concat_axis=1, tiled=True)
    spatial_keep = position_ids[None, :] < live_positions
    spatial_out = attend(
        spatial[0], spatial[1], spatial[2], spatial_keep, "bqhd,bkhd->bhqk", "bhqk,bkhd->bqhd"
    ).astype(jnp.bfloat16)
    total_frames = exchanged.shape[1]
    slice_positions = exchanged.shape[2]
    temporal_keep = jnp.broadcast_to(
        jnp.arange(total_frames, dtype=jnp.int32)[None, :] < live_frames,
        (slice_positions, total_frames),
    )

    def temporal_attend(queries, key_block, value_block):
        return attend(
            queries, key_block, value_block, temporal_keep, "qbhd,kbhd->bhqk", "bhqk,kbhd->qbhd"
        )

    temporal_result, pullback = jax.vjp(temporal_attend, exchanged[0], exchanged[1], exchanged[2])
    temporal_out = temporal_result.astype(jnp.bfloat16)
    input_grads = jnp.stack(pullback(exchanged[3].astype(jnp.float32)))
    temporal_frames = lax.all_to_all(temporal_out, "seq", split_axis=0, concat_axis=1, tiled=True)
    grads_home = lax.all_to_all(input_grads, "seq", split_axis=1, concat_axis=2, tiled=True)
    tokens = frame_count * position_count
    flat_spatial = spatial_out.reshape(tokens, width)
    flat_temporal = temporal_frames.reshape(tokens, width)
    slice_width = width // group_size
    column_spatial, column_temporal = (
        lax.all_to_all(flat_spatial, "seq", split_axis=1, concat_axis=0, tiled=True),
        lax.all_to_all(flat_temporal, "seq", split_axis=1, concat_axis=0, tiled=True),
    )
    spatial_scale = spatial_gate[0]
    temporal_scale = temporal_gate[0]
    starting = jnp.zeros((slice_width, 2, width), jnp.float32)
    cot_piece = lax.all_gather(incoming.reshape(tokens, width), "seq", axis=0, tiled=True)
    shards = cot_piece.shape[0] // tokens

    def one_block(block, total):
        offset = (block * tokens).astype(jnp.int32)
        rows = lax.dynamic_slice_in_dim(cot_piece, offset, tokens, 0)
        token_index = offset + jnp.arange(tokens, dtype=jnp.int32)
        frame_of = token_index // position_count
        position_of = token_index % position_count
        row_keep = ((frame_of < live_frames) & (position_of < live_positions)).astype(jnp.float32)
        masked_rows = row_keep[:, None] * rows.astype(jnp.float32)
        error_first = (masked_rows * spatial_scale).astype(jnp.bfloat16)
        error_second = (masked_rows * temporal_scale).astype(jnp.bfloat16)
        cols_first = lax.dynamic_slice_in_dim(column_spatial, offset, tokens, 0)
        cols_second = lax.dynamic_slice_in_dim(column_temporal, offset, tokens, 0)
        part_first = lax.dot_general(
            cols_first, error_first, (((0,), (0,)), ((), ())), preferred_element_type=jnp.float32
        )
        part_second = lax.dot_general(
            cols_second, error_second, (((0,), (0,)), ((), ())), preferred_element_type=jnp.float32
        )
        part_first = part_first.astype(jnp.bfloat16).astype(jnp.float32)
        part_second = part_second.astype(jnp.bfloat16).astype(jnp.float32)
        return total + jnp.stack([part_first, part_second], axis=1)

    partial_sum = lax.fori_loop(0, shards, one_block, starting)
    summed = lax.psum_scatter(partial_sum, "dp", scatter_dimension=2, tiled=True)
    return (grads_home[None], summed[:, 0], summed[:, 1])


def kernel(
    n, nb, units, counts, sgate, tgate, sqkv_hbm, tqkv_hbm, cot_hbm, proj_hbm,
    g_out, sum_out,
    sqkv, tqkv, cot, proj, cot_t, sg_t, tg_t, q_t, v_t, o_t, so, so_r, tq, tq_r, tq2_r, tqf,
    err, err2, ot, do_t, slf, sl_s, sl_r, part, xr, zs, zr, gs, gr,
    loc_sem, cs, cr, fs, fr, ss, sr, ts, tr, vs, vr, ls, lr, us, ur, xss, xrs, zss, zrs,
):
    me = lax.axis_index("seq")
    dp = lax.axis_index("dp")
    pos, width = cot.shape
    sl = width // n
    rows = width // nb
    pieces = tq.shape[1]
    half = sl // pieces
    heads = half // HD
    outer = nb // 2
    y, c = me // 2, me % 2
    first_frame = 2 * y
    mate = first_frame + 1 - c
    twin = (me + 2) % n
    cross = (mate + 2) % n
    oz, ox = dp // 2, dp % 2
    scale = HD ** (-0.5)

    loads = [
        pltpu.make_async_copy(cot_hbm, cot, loc_sem.at[0]),
        pltpu.make_async_copy(sqkv_hbm, sqkv, loc_sem.at[1]),
        pltpu.make_async_copy(tqkv_hbm, tqkv, loc_sem.at[2]),
        pltpu.make_async_copy(proj_hbm.at[me], proj.at[0], loc_sem.at[3]),
        pltpu.make_async_copy(proj_hbm.at[twin], proj.at[1], loc_sem.at[4]),
    ]
    for load in loads:
        load.start()
    barrier = pltpu.get_barrier_semaphore()
    for j in range(1, n):
        pl.semaphore_signal(barrier, inc=1, device_id=(dp, (me + j) % n), device_id_type=MESH)
    pl.semaphore_signal(barrier, inc=1, device_id=(oz * 2 + 1 - ox, me), device_id_type=MESH)
    for j in range(1, outer):
        pl.semaphore_signal(
            barrier, inc=1, device_id=((oz + j) % outer * 2 + ox, me), device_id_type=MESH
        )

    def remote(src, dst, s_sem, r_sem, to):
        return pltpu.make_async_remote_copy(
            src_ref=src, dst_ref=dst, send_sem=s_sem, recv_sem=r_sem, device_id=to,
            device_id_type=MESH,
        )

    def turned(value):
        return value.astype(F32).T

    sent = []

    def send(copy):
        copy.start()
        sent.append(copy)

    partners = [(twin, 2 + c, 2 + c), (cross, 2 + c, 3 - c), (mate, c, 1 - c)]

    loads[0].wait()
    flat = turned(cot[...]).astype(BF16)
    for d in range(nb):
        cot_t[c, (d + ox + 1) % 2, d // 2] = flat[d * rows : (d + 1) * rows, :]
    pl.semaphore_wait(barrier, (n - 1) + 1 + (outer - 1))

    def cot_y(h):
        return remote(cot_t.at[c, h], cot_t.at[2 + c, h], cs.at[h], cr.at[h], (dp, twin))

    def cot_mate(h, k, core):
        slot = 2 * k + core
        return remote(cot_t.at[slot, h], cot_t.at[slot, h], fs.at[k, h], fr.at[k, h], (dp, mate))

    def cot_y_arrived(h):
        remote(cot_t.at[c, h], cot_t.at[2 + c, h], cs.at[h], cr.at[h], (dp, twin)).wait_recv()

    send(cot_y(0))
    for h in range(2):
        send(cot_mate(h, 0, c))

    live_frames = counts[0, 0]
    live_positions = counts[0, 1]

    loads[1].wait()
    q_t[...] = turned(sqkv[0])
    v_t[...] = turned(sqkv[2])
    key_keep = lax.broadcasted_iota(jnp.int32, (pos, pos), 0) < live_positions
    for h in range(HEADS):
        low = h * HD
        w0 = low // 128 * 128
        w1 = -(-(low + HD) // 128) * 128
        row = lax.broadcasted_iota(jnp.int32, (w1 - w0, pos), 0)
        inside = (row >= low - w0) & (row < low - w0 + HD)
        q_win = jnp.where(inside, q_t[w0:w1, :], 0.0).astype(BF16)
        scores = jnp.dot(sqkv[1, :, w0:w1], q_win, preferred_element_type=F32) * scale
        scores = jnp.where(key_keep, scores, -1e30)
        expo = jnp.exp(scores - jnp.max(scores, axis=0, keepdims=True))
        weights = (expo / jnp.sum(expo, axis=0, keepdims=True)).astype(BF16)
        o_t[low : low + HD, :] = jnp.dot(
            v_t[low : low + HD, :].astype(BF16), weights, preferred_element_type=F32
        )
    for s in range(n):
        so[s] = o_t[s * sl : (s + 1) * sl, :].astype(BF16)

    def so_copy(k):
        to, there, _ = partners[k]
        return remote(so.at[to], so_r.at[there], ss.at[k], sr.at[k], (dp, to))

    def so_arrived(k):
        to, _, here = partners[k]
        remote(so.at[to], so_r.at[here], ss.at[k], sr.at[k], (dp, to)).wait_recv()

    for k in range(3):
        send(so_copy(k))
    send(cot_y(1))
    so_r[c] = so[me]

    loads[2].wait()
    for m in range(3):
        flat = turned(tqkv[m]).astype(BF16)
        for s in range(n):
            for i in range(pieces):
                low = s * sl + i * half
                tq[s, i, m] = flat[low : low + half, :]

    def near_copy(k, i):
        to, there, _ = partners[k]
        return remote(tq.at[to, i], tq_r.at[there, i], ts.at[i, k], tr.at[i, k], (dp, to))

    def near_arrived(i):
        for k in range(3):
            to, _, here = partners[k]
            remote(
                tq.at[to, i], tq_r.at[here, i], ts.at[i, k], tr.at[i, k], (dp, to)
            ).wait_recv()

    def far_copy(k, i):
        to, there, _ = partners[k]
        return remote(
            tq.at[(to + 2) % n, i, :2], tq2_r.at[there, i], vs.at[i, k], vr.at[i, k], (dp, to)
        )

    def far_arrived(i):
        for k in range(3):
            to, _, here = partners[k]
            remote(
                tq.at[(to + 2) % n, i, :2], tq2_r.at[here, i], vs.at[i, k], vr.at[i, k], (dp, to)
            ).wait_recv()

    for i in range(pieces):
        for k in range(3):
            send(near_copy(k, i))
    for i in range(pieces):
        send(far_copy(2, i))
        if i < pieces - 1:
            send(far_copy(0, i))
            send(far_copy(1, i))
    tq_r[c] = tq[me]
    for i in range(pieces):
        tq2_r[c, i] = tq[twin, i, :2]

    sg_t[...] = jnp.broadcast_to(sgate[...], (pos, width)).T
    tg_t[...] = jnp.broadcast_to(tgate[...], (pos, width)).T
    lane = lax.broadcasted_iota(jnp.int32, (1, pos), 1)
    frame_live = [(f + first_frame) % n < live_frames for f in range(n)]
    keep = [((lane < live_positions) & frame_live[f]).astype(F32) for f in range(n)]

    def errors(target, gate, h):
        for z in range(outer):
            at = pl.ds(pl.multiple_of((z * 2 + (1 - ox if h == 0 else ox)) * rows, 16), rows)
            column = gate[at, :]
            for f in range(n):
                target[at, f * pos : (f + 1) * pos] = (
                    keep[f] * cot_t[f, h, z].astype(F32) * column
                ).astype(BF16)

    def cot_arrived(h):
        cot_y_arrived(h)
        send(cot_mate(h, 1, c))
        for k in range(2):
            cot_mate(h, k, 1 - c).wait_recv()

    order = list(range(1, outer)) + [0]

    def times(left, right):
        return lax.dot_general(left, right, (((1,), (1,)), ((), ())), preferred_element_type=F32)

    def product(p, source, outs, h):
        main, tail, groups, _ = units[p]
        x = 1 - ox if h == 0 else ox
        if tail:
            short = rows // groups
            edges = []
            for k in range(groups):
                blank = [
                    jnp.zeros((size, outs.shape[1]), BF16)
                    for size in (k * tail, 128 - (k + 1) * tail)
                ]
                parts = [blank[0], outs[main:, :], blank[1]]
                edges.append(jnp.concatenate([v for v in parts if v.shape[0]], axis=0))
        for j in order:
            d = (oz + j) % outer * 2 + x
            first = pl.multiple_of(d * rows, 16)
            wide = times(source[pl.ds(first, rows), :], outs[:main, :]).astype(BF16)
            for k in range(main // 128):
                part[p, d, k * rows : (k + 1) * rows, :] = wide[:, k * 128 : (k + 1) * 128]
            if tail:
                edge = functools.reduce(
                    jnp.add,
                    [
                        times(
                            source[pl.ds(pl.multiple_of(first + k * short, 16), short), :],
                            edges[k],
                        )
                        for k in range(groups)
                    ],
                )
                part[p, d, main // 128 * rows : units[p][3], :] = edge.astype(BF16)
            if h == 0:
                send(pair_copy(p, j))

    def pair_copy(p, j):
        z = (oz + j) % outer
        size = units[p][3]
        return remote(
            part.at[p, z * 2 + 1 - ox, :size], xr.at[p, j, :size], xss.at[p, j], xrs.at[p, j],
            (oz * 2 + 1 - ox, me),
        )

    def line_copy(p, j):
        z = (oz + j) % outer
        size = units[p][3]
        return remote(
            zs.at[p, j - 1, :size], zr.at[p, j - 1, :size],
            zss.at[p, j - 1], zrs.at[p, j - 1], (z * 2 + ox, me)
        )

    def line_start(p, j):
        z = (oz + j) % outer
        pair_copy(p, j).wait_recv()
        size = units[p][3]
        zs[p, j - 1, :size, :] = (
            part[p, z * 2 + ox, :size, :].astype(F32) + xr[p, j, :size, :].astype(F32)
        ).astype(BF16)
        send(line_copy(p, j))

    def line_end(p):
        size = units[p][3]
        pair_copy(p, 0).wait_recv()
        total = part[p, oz * 2 + ox, :size, :].astype(F32) + xr[p, 0, :size, :].astype(F32)
        for j in range(1, outer):
            line_copy(p, j).wait_recv()
            total = total + zr[p, j - 1, :size, :].astype(F32)
        sum_out[p, :size, :] = total

    cot_arrived(0)
    errors(err, sg_t, 0)
    errors(err2, tg_t, 0)
    for k in range(3):
        so_arrived(k)
    spatial_rows = jnp.concatenate([so_r[f] for f in range(n)], axis=1)
    product(0, err, spatial_rows, 0)
    cot_arrived(1)
    errors(err, sg_t, 1)
    product(0, err, spatial_rows, 1)
    errors(err2, tg_t, 1)
    loads[3].wait()
    loads[4].wait()
    for b in range(2):
        do_t[b] = (
            jnp.dot(proj[b], err2[...], preferred_element_type=F32).astype(BF16).astype(F32)
        )

    def forward(i):
        kept = []
        for f in range(n):
            for m in range(3):
                tqf[f, i, m] = tq_r[f, i, m].astype(F32)
        for h in range(heads):
            band = slice(h * HD, (h + 1) * HD)
            place = slice(i * half + h * HD, i * half + (h + 1) * HD)
            keys = [tqf[g, i, 1, band, :] for g in range(n)]
            values = [tqf[g, i, 2, band, :] for g in range(n)]
            for f in range(n):
                q = tqf[f, i, 0, band, :]
                row = [
                    jnp.where(
                        frame_live[g], jnp.sum(q * keys[g], axis=0, keepdims=True) * scale, -1e30
                    )
                    for g in range(n)
                ]
                top = functools.reduce(jnp.maximum, row)
                expo = [jnp.exp(value - top) for value in row]
                total = functools.reduce(jnp.add, expo)
                soft = [value / total for value in expo]
                rounded = [value.astype(BF16).astype(F32) for value in soft]
                kept.append((soft, rounded))
                ot[place, f * pos : (f + 1) * pos] = functools.reduce(
                    jnp.add, [rounded[g] * values[g] for g in range(n)]
                ).astype(BF16)
        return kept

    def rows_sent(slopes, weights):
        there = lambda table, a, b: table[(a + 2) % n][(b + 2) % n]
        out = [there(slopes, a, b) for a in range(2) for b in range(n)]
        out += [there(slopes, a, b) for a in range(2, n) for b in range(2)]
        return out + [there(weights, a, b) for a in range(n) for b in range(2)]

    def slopes_copy(i):
        return remote(sl_s.at[i], sl_r.at[i], ls.at[i], lr.at[i], (dp, twin))

    def back_copy(b, i):
        return remote(
            gs.at[1 - c, b, i], gr.at[b, i], us.at[b, i], ur.at[b, i], (dp, mate)
        )

    def add(values):
        return functools.reduce(jnp.add, values)

    def backward(i, kept):
        all_slopes = []
        for h in range(heads):
            band = slice(h * HD, (h + 1) * HD)
            place = slice(i * half + h * HD, i * half + (h + 1) * HD)
            backs = [do_t[0, place, f * pos : (f + 1) * pos] for f in range(n)]
            slopes = []
            for f in range(n):
                soft, _ = kept[h * n + f]
                dw = [
                    jnp.sum(backs[f] * tqf[g, i, 2, band, :], axis=0, keepdims=True)
                    .astype(BF16)
                    .astype(F32)
                    for g in range(n)
                ]
                mean = add([soft[g] * dw[g] for g in range(n)])
                slopes.append([soft[g] * (dw[g] - mean) * scale for g in range(n)])
            all_slopes.append(slopes)
            weights = [kept[h * n + f][1] for f in range(n)]
            out = rows_sent(slopes, weights)
            for k, value in enumerate(out):
                at = h * len(out) + k
                slf[i, at : at + 1, :] = value
        used = heads * len(out)
        if used < slf.shape[1]:
            slf[i, used:, :] = jnp.zeros((slf.shape[1] - used, pos), F32)
        sl_s[i] = slf[i].astype(BF16)
        send(slopes_copy(i))
        for h in range(heads):
            band = slice(h * HD, (h + 1) * HD)
            place = slice(i * half + h * HD, i * half + (h + 1) * HD)
            slopes = all_slopes[h]
            for f in range(2):
                gs[f, 0, i, 0, band, :] = add(
                    [slopes[f][g] * tqf[g, i, 1, band, :] for g in range(n)]
                ).astype(BF16)
                gs[f, 0, i, 1, band, :] = add(
                    [slopes[g][f] * tqf[g, i, 0, band, :] for g in range(n)]
                ).astype(BF16)
                gs[f, 0, i, 2, band, :] = add(
                    [
                        kept[h * n + g][1][f] * do_t[0, place, g * pos : (g + 1) * pos]
                        for g in range(n)
                    ]
                ).astype(BF16)
        send(back_copy(0, i))

    def far_backward(i):
        slopes_copy(i).wait_recv()
        far_arrived(i)
        table = sl_r[i].astype(F32)
        for h in range(heads):
            band = slice(h * HD, (h + 1) * HD)
            place = slice(i * half + h * HD, i * half + (h + 1) * HD)
            at = h * (8 * n - 12)
            row = lambda k: table[at + k : at + k + 1, :]
            for f in range(2):
                along = [row(f * n + g) for g in range(n)]
                down = [row(g * n + f) if g < 2 else row(2 * n + (g - 2) * 2 + f) for g in range(n)]
                mixed = [row(4 * n - 4 + g * 2 + f) for g in range(n)]
                gs[f, 1, i, 0, band, :] = add(
                    [along[g] * tq2_r[g, i, 1, band, :].astype(F32) for g in range(n)]
                ).astype(BF16)
                gs[f, 1, i, 1, band, :] = add(
                    [down[g] * tq2_r[g, i, 0, band, :].astype(F32) for g in range(n)]
                ).astype(BF16)
                gs[f, 1, i, 2, band, :] = add(
                    [mixed[g] * do_t[1, place, g * pos : (g + 1) * pos] for g in range(n)]
                ).astype(BF16)
        send(back_copy(1, i))

    starts = [0]
    for unit in units[1:]:
        starts.append(starts[-1] + unit[0] + unit[1])
    for j in range(1, outer):
        line_start(0, j)
    for i in range(pieces):
        near_arrived(i)
        kept = forward(i)
        outs = ot[starts[i] : starts[i + 1], :]
        for h in range(2):
            product(1 + i, err2, outs, h)
        backward(i, kept)
        if i == pieces - 1:
            send(far_copy(0, i))
            send(far_copy(1, i))
        else:
            for j in range(1, outer):
                line_start(1 + i, j)
    line_end(0)
    last = pieces
    for i in range(pieces - 1):
        far_backward(i)
        line_end(1 + i)
    for j in range(1, outer):
        line_start(last, j)
    far_backward(pieces - 1)
    for b in range(2):
        for i in range(pieces):
            back_copy(b, i).wait_recv()
    for m in range(3):
        for b in range(2):
            for i in range(pieces):
                for block, source in ((me + 2 * b, gs.at[c]), (mate + 2 * b, gr)):
                    low = pl.multiple_of(block % n * sl + i * half, 16)
                    q_t[pl.ds(low, half), :] = source[b, i, m].astype(F32)
        g_out[m] = q_t[...].T.astype(BF16)
    line_end(last)
    for copy in sent:
        copy.wait_send()


def finish(units, grads, sums, g_out, sp_out, tp_out):
    g_out[...] = grads[...]
    rows = sp_out.shape[0]

    @pl.when(pl.program_id(0) == 0)
    def _():
        left = 0
        for p, (main, tail, groups, size) in enumerate(units):
            out = tp_out if p else sp_out
            for k in range(main // 128):
                low = left + k * 128
                out[:, low : low + 128] = sums[p, k * rows : (k + 1) * rows, :]
            if tail:
                short = rows // groups
                edge = sums[p, main // 128 * rows : size, :]
                low = left + main
                for k in range(groups):
                    out[k * short : (k + 1) * short, low : low + tail] = edge[
                        :, k * tail : (k + 1) * tail
                    ]
            left = left + main + tail if p else 0


def unit_of(columns, rows):
    main, tail = columns // 128 * 128, columns % 128
    groups = 1
    if tail:
        groups = max(g for g in range(1, 128 // tail + 1) if rows % (16 * g) == 0)
    return main, tail, groups, main // 128 * rows + (rows // groups if tail else 0)


def kernel_body(
    n, nb, spatial_qkv, temporal_qkv, cotangent, spatial_gate, temporal_gate, temporal_proj, live_counts
):
    pos, width = cotangent.shape[2:]
    sl, rows, outer = width // n, width // nb, nb // 2
    vm, dma = pltpu.VMEM, pltpu.SemaphoreType.DMA
    whole = pl.BlockSpec(memory_space=pltpu.VMEM)
    left = pl.BlockSpec(memory_space=pl.ANY)
    pieces = 2 if sl // HD % 2 == 0 and sl // 2 % 16 == 0 else 1
    half = sl // pieces
    cut = half // 128 * 128
    columns = [cut, sl - cut] if pieces == 2 and cut else [half] * pieces
    units = [unit_of(size, rows) for size in [sl] + columns]
    count, packed = len(units), max(unit[3] for unit in units)
    table = -(-(half // HD * (8 * n - 12)) // 16) * 16
    grads, sums = pl.pallas_call(
        functools.partial(kernel, n, nb, units),
        out_shape=(
            jax.ShapeDtypeStruct((3, pos, width), BF16),
            jax.ShapeDtypeStruct((count, packed, 128), F32),
        ),
        in_specs=[pl.BlockSpec(memory_space=pltpu.SMEM), whole, whole, left, left, left, left],
        out_specs=(whole, whole),
        scratch_shapes=[
            vm((3, pos, width), BF16), vm((3, pos, width), BF16), vm((pos, width), BF16),
            vm((2, sl, width), BF16), vm((n, 2, outer, rows, pos), BF16),
            vm((width, pos), F32), vm((width, pos), F32),
            vm((width, pos), F32), vm((width, pos), F32), vm((width, pos), F32),
            vm((n, sl, pos), BF16), vm((n, sl, pos), BF16),
            vm((n, pieces, 3, half, pos), BF16), vm((n, pieces, 3, half, pos), BF16),
            vm((n, pieces, 2, half, pos), BF16), vm((n, pieces, 3, half, pos), F32),
            vm((width, n * pos), BF16), vm((width, n * pos), BF16),
            vm((sl, n * pos), BF16), vm((2, sl, n * pos), F32),
            vm((pieces, table, pos), F32), vm((pieces, table, pos), BF16),
            vm((pieces, table, pos), BF16),
            vm((count, nb, packed, 128), BF16), vm((count, outer, packed, 128), BF16),
            vm((count, outer - 1, packed, 128), BF16), vm((count, outer - 1, packed, 128), BF16),
            vm((2, 2, pieces, 3, half, pos), BF16), vm((2, pieces, 3, half, pos), BF16),
            dma((5,)), dma((2,)), dma((2,)), dma((2, 2)), dma((2, 2)),
            dma((3,)), dma((3,)), dma((pieces, 3)), dma((pieces, 3)),
            dma((pieces, 3)), dma((pieces, 3)), dma((pieces,)), dma((pieces,)),
            dma((2, pieces)), dma((2, pieces)),
            dma((count, outer)), dma((count, outer)), dma((count, outer - 1)), dma((count, outer - 1)),
        ],
        compiler_params=pltpu.CompilerParams(
            collective_id=0, has_side_effects=True, vmem_limit_bytes=56 * 1024 * 1024
        ),
    )(
        live_counts, spatial_gate, temporal_gate,
        spatial_qkv.reshape(3, pos, width), temporal_qkv.reshape(3, pos, width),
        cotangent.reshape(pos, width), temporal_proj.reshape(n, sl, width),
    )
    fixed = lambda i: (0, 0)
    grads, first, second = pl.pallas_call(
        functools.partial(finish, units),
        grid=(1,),
        out_shape=(
            jax.ShapeDtypeStruct((3, pos, width), BF16),
            jax.ShapeDtypeStruct((rows, sl), F32),
            jax.ShapeDtypeStruct((rows, sl), F32),
        ),
        in_specs=[
            pl.BlockSpec((3, pos, width), lambda i: (0, 0, 0)),
            pl.BlockSpec((count, packed, 128), lambda i: (0, 0, 0)),
        ],
        out_specs=(
            pl.BlockSpec((3, pos, width), lambda i: (0, 0, 0)),
            pl.BlockSpec((rows, sl), fixed),
            pl.BlockSpec((rows, sl), fixed),
        ),
    )(grads, sums)
    return grads[None, :, None], first.T, second.T


def solution(mesh):
    n, nb = mesh.shape["seq"], mesh.shape["dp"]

    def chosen(*args):
        cot = args[2]
        _, frames, pos, width = cot.shape
        fits = frames == 1 and pos == 128 and width == HEADS * HD and n % 2 == 0 and nb % 2 == 0
        fits = fits and n == 4 and nb > 2 and HEADS % n == 0
        if fits and width // n % 16 == 0 and width // nb % 16 == 0:
            return kernel_body(n, nb, *args)
        return body(*args)

    return jax.shard_map(
        chosen,
        mesh=mesh,
        in_specs=(
            P("dp", None, "seq", None, None),
            P("dp", None, "seq", None, None),
            P("dp", "seq", None, None),
            P("dp", None),
            P("dp", None),
            P(),
            P("dp", None),
        ),
        out_specs=(P("dp", None, "seq", None, None), P("seq", "dp"), P("seq", "dp")),
        check_vma=False,
    )
```

```python
import functools

import jax
import jax.numpy as jnp
from jax import lax
from jax.experimental import pallas as pl
from jax.experimental.pallas import tpu as pltpu
from jax.sharding import PartitionSpec as P

HEADS = 16
HD = 72
MESH = pl.DeviceIdType.MESH
F32 = jnp.float32
BF16 = jnp.bfloat16


def attend(queries, key_block, value_block, key_keep, score_form, mix_form):
    head_split = queries.shape[:-1] + (HEADS, HD)
    q_heads = queries.reshape(head_split)
    k_heads = key_block.reshape(head_split)
    v_heads = value_block.reshape(head_split)
    scores = jnp.einsum(score_form, q_heads, k_heads, preferred_element_type=jnp.float32) * HD ** (
        -0.5
    )
    scores = jnp.where(key_keep[:, None, None, :], scores, -1e30)
    shifted = scores - jnp.max(scores, axis=-1, keepdims=True)
    expo = jnp.exp(shifted)
    attention_weights = (expo / jnp.sum(expo, axis=-1, keepdims=True)).astype(jnp.bfloat16)
    mixed = jnp.einsum(mix_form, attention_weights, v_heads, preferred_element_type=jnp.float32)
    return mixed.reshape(queries.shape)


def body(
    spatial_qkv, temporal_qkv, cotangent, spatial_gate, temporal_gate, temporal_proj, live_counts
):
    spatial = spatial_qkv[0]
    temporal = temporal_qkv[0]
    incoming = cotangent[0]
    frame_count, position_count, width = incoming.shape
    group_size = lax.axis_size("seq")
    member = lax.axis_index("seq")
    live_frames = live_counts[0, 0]
    live_positions = live_counts[0, 1]
    frame_ids = member * frame_count + jnp.arange(frame_count, dtype=jnp.int32)
    position_ids = jnp.arange(position_count, dtype=jnp.int32)
    token_mask = (
        (frame_ids[:, None] < live_frames) & (position_ids[None, :] < live_positions)
    ).astype(jnp.float32)
    flowing = token_mask[:, :, None] * incoming.astype(jnp.float32)
    temporal_error = (flowing * temporal_gate[0]).astype(jnp.bfloat16)
    temporal_back = lax.dot_general(
        temporal_error, temporal_proj, (((2,), (1,)), ((), ())), preferred_element_type=jnp.float32
    ).astype(jnp.bfloat16)
    stacked = jnp.concatenate([temporal, temporal_back[None]], axis=0)
    exchanged = lax.all_to_all(stacked, "seq", split_axis=2, concat_axis=1, tiled=True)
    spatial_keep = position_ids[None, :] < live_positions
    spatial_out = attend(
        spatial[0], spatial[1], spatial[2], spatial_keep, "bqhd,bkhd->bhqk", "bhqk,bkhd->bqhd"
    ).astype(jnp.bfloat16)
    total_frames = exchanged.shape[1]
    slice_positions = exchanged.shape[2]
    temporal_keep = jnp.broadcast_to(
        jnp.arange(total_frames, dtype=jnp.int32)[None, :] < live_frames,
        (slice_positions, total_frames),
    )

    def temporal_attend(queries, key_block, value_block):
        return attend(
            queries, key_block, value_block, temporal_keep, "qbhd,kbhd->bhqk", "bhqk,kbhd->qbhd"
        )

    temporal_result, pullback = jax.vjp(temporal_attend, exchanged[0], exchanged[1], exchanged[2])
    temporal_out = temporal_result.astype(jnp.bfloat16)
    input_grads = jnp.stack(pullback(exchanged[3].astype(jnp.float32)))
    temporal_frames = lax.all_to_all(temporal_out, "seq", split_axis=0, concat_axis=1, tiled=True)
    grads_home = lax.all_to_all(input_grads, "seq", split_axis=1, concat_axis=2, tiled=True)
    tokens = frame_count * position_count
    flat_spatial = spatial_out.reshape(tokens, width)
    flat_temporal = temporal_frames.reshape(tokens, width)
    slice_width = width // group_size
    column_spatial, column_temporal = (
        lax.all_to_all(flat_spatial, "seq", split_axis=1, concat_axis=0, tiled=True),
        lax.all_to_all(flat_temporal, "seq", split_axis=1, concat_axis=0, tiled=True),
    )
    spatial_scale = spatial_gate[0]
    temporal_scale = temporal_gate[0]
    starting = jnp.zeros((slice_width, 2, width), jnp.float32)
    cot_piece = lax.all_gather(incoming.reshape(tokens, width), "seq", axis=0, tiled=True)
    shards = cot_piece.shape[0] // tokens

    def one_block(block, total):
        offset = (block * tokens).astype(jnp.int32)
        rows = lax.dynamic_slice_in_dim(cot_piece, offset, tokens, 0)
        token_index = offset + jnp.arange(tokens, dtype=jnp.int32)
        frame_of = token_index // position_count
        position_of = token_index % position_count
        row_keep = ((frame_of < live_frames) & (position_of < live_positions)).astype(jnp.float32)
        masked_rows = row_keep[:, None] * rows.astype(jnp.float32)
        error_first = (masked_rows * spatial_scale).astype(jnp.bfloat16)
        error_second = (masked_rows * temporal_scale).astype(jnp.bfloat16)
        cols_first = lax.dynamic_slice_in_dim(column_spatial, offset, tokens, 0)
        cols_second = lax.dynamic_slice_in_dim(column_temporal, offset, tokens, 0)
        part_first = lax.dot_general(
            cols_first, error_first, (((0,), (0,)), ((), ())), preferred_element_type=jnp.float32
        )
        part_second = lax.dot_general(
            cols_second, error_second, (((0,), (0,)), ((), ())), preferred_element_type=jnp.float32
        )
        part_first = part_first.astype(jnp.bfloat16).astype(jnp.float32)
        part_second = part_second.astype(jnp.bfloat16).astype(jnp.float32)
        return total + jnp.stack([part_first, part_second], axis=1)

    partial_sum = lax.fori_loop(0, shards, one_block, starting)
    summed = lax.psum_scatter(partial_sum, "dp", scatter_dimension=2, tiled=True)
    return (grads_home[None], summed[:, 0], summed[:, 1])


def kernel(
    n, nb, units, counts_hbm, sgate_hbm, tgate_hbm, sqkv_hbm, tqkv_hbm, cot_hbm, proj_hbm,
    g_hbm, sum_hbm,
    counts, sgate, tgate, g_out, sum_out, out_sem, sqkv, tqkv, cot, proj, cot_t, sg_t, tg_t, q_t, v_t, o_t, so, so_r, tq, tq_r, tq2_r, tqf,
    err, err2, ot, do_t, slf, sl_s, sl_r, part, xr, zs, zr, gs, gr, g_t,
    loc_sem, cs, cr, fs, fr, ss, sr, ts, tr, vs, vr, ls, lr, us, ur, xss, xrs, zss, zrs,
):
    me = lax.axis_index("seq")
    dp = lax.axis_index("dp")
    pos, width = cot.shape
    sl = width // n
    rows = width // nb
    pieces = tq.shape[1]
    half = sl // pieces
    heads = half // HD
    outer = nb // 2
    y, c = me // 2, me % 2
    first_frame = 2 * y
    mate = first_frame + 1 - c
    twin = (me + 2) % n
    cross = (mate + 2) % n
    oz, ox = dp // 2, dp % 2
    scale = HD ** (-0.5)

    loads = [
        pltpu.make_async_copy(cot_hbm, cot, loc_sem.at[0]),
        pltpu.make_async_copy(sqkv_hbm, sqkv, loc_sem.at[1]),
        pltpu.make_async_copy(tqkv_hbm, tqkv, loc_sem.at[2]),
        pltpu.make_async_copy(proj_hbm.at[me], proj.at[0], loc_sem.at[3]),
        pltpu.make_async_copy(proj_hbm.at[twin], proj.at[1], loc_sem.at[4]),
        pltpu.make_async_copy(counts_hbm, counts, loc_sem.at[5]),
        pltpu.make_async_copy(sgate_hbm, sgate, loc_sem.at[6]),
        pltpu.make_async_copy(tgate_hbm, tgate, loc_sem.at[7]),
    ]
    loads[0].start()
    barrier = pltpu.get_barrier_semaphore()
    for j in range(1, n):
        pl.semaphore_signal(barrier, inc=1, device_id=(dp, (me + j) % n), device_id_type=MESH)
    pl.semaphore_signal(barrier, inc=1, device_id=(oz * 2 + 1 - ox, me), device_id_type=MESH)
    for j in range(1, outer):
        pl.semaphore_signal(
            barrier, inc=1, device_id=((oz + j) % outer * 2 + ox, me), device_id_type=MESH
        )

    for load in loads[5:] + loads[1:5]:
        load.start()

    def remote(src, dst, s_sem, r_sem, to):
        return pltpu.make_async_remote_copy(
            src_ref=src, dst_ref=dst, send_sem=s_sem, recv_sem=r_sem, device_id=to,
            device_id_type=MESH,
        )

    def turned(value):
        return value.astype(F32).T

    sent = []

    def send(copy):
        copy.start()
        sent.append(copy)

    partners = [(twin, 2 + c, 2 + c), (cross, 2 + c, 3 - c), (mate, c, 1 - c)]

    loads[0].wait()
    flat = turned(cot[...]).astype(BF16)
    for d in range(nb):
        cot_t[c, (d + ox + 1) % 2, d // 2] = flat[d * rows : (d + 1) * rows, :]
    pl.semaphore_wait(barrier, (n - 1) + 1 + (outer - 1))

    def cot_y(h):
        return remote(cot_t.at[c, h], cot_t.at[2 + c, h], cs.at[h], cr.at[h], (dp, twin))

    def cot_mate(h, k, core):
        slot = 2 * k + core
        return remote(cot_t.at[slot, h], cot_t.at[slot, h], fs.at[k, h], fr.at[k, h], (dp, mate))

    def cot_y_arrived(h):
        remote(cot_t.at[c, h], cot_t.at[2 + c, h], cs.at[h], cr.at[h], (dp, twin)).wait_recv()

    send(cot_y(0))
    for h in range(2):
        send(cot_mate(h, 0, c))

    loads[5].wait()
    live_frames = counts[0, 0]
    live_positions = counts[0, 1]

    loads[1].wait()
    q_t[...] = turned(sqkv[0])
    v_t[...] = turned(sqkv[2])
    key_keep = lax.broadcasted_iota(jnp.int32, (pos, pos), 0) < live_positions
    for h in range(HEADS):
        low = h * HD
        w0 = low // 128 * 128
        w1 = -(-(low + HD) // 128) * 128
        row = lax.broadcasted_iota(jnp.int32, (w1 - w0, pos), 0)
        inside = (row >= low - w0) & (row < low - w0 + HD)
        q_win = jnp.where(inside, q_t[w0:w1, :], 0.0).astype(BF16)
        scores = jnp.dot(sqkv[1, :, w0:w1], q_win, preferred_element_type=F32) * scale
        scores = jnp.where(key_keep, scores, -1e30)
        expo = jnp.exp(scores - jnp.max(scores, axis=0, keepdims=True))
        weights = (expo / jnp.sum(expo, axis=0, keepdims=True)).astype(BF16)
        o_t[low : low + HD, :] = jnp.dot(
            v_t[low : low + HD, :].astype(BF16), weights, preferred_element_type=F32
        )
    for s in range(n):
        so[s] = o_t[s * sl : (s + 1) * sl, :].astype(BF16)

    def so_copy(k):
        to, there, _ = partners[k]
        return remote(so.at[to], so_r.at[there], ss.at[k], sr.at[k], (dp, to))

    def so_arrived(k):
        to, _, here = partners[k]
        remote(so.at[to], so_r.at[here], ss.at[k], sr.at[k], (dp, to)).wait_recv()

    for k in range(3):
        send(so_copy(k))
    send(cot_y(1))
    so_r[c] = so[me]

    loads[2].wait()
    for m in range(3):
        flat = turned(tqkv[m]).astype(BF16)
        for s in range(n):
            for i in range(pieces):
                low = s * sl + i * half
                tq[s, i, m] = flat[low : low + half, :]

    def near_copy(k, i):
        to, there, _ = partners[k]
        return remote(tq.at[to, i], tq_r.at[there, i], ts.at[i, k], tr.at[i, k], (dp, to))

    def near_arrived(i):
        for k in range(3):
            to, _, here = partners[k]
            remote(
                tq.at[to, i], tq_r.at[here, i], ts.at[i, k], tr.at[i, k], (dp, to)
            ).wait_recv()

    def far_copy(k, i):
        to, there, _ = partners[k]
        return remote(
            tq.at[(to + 2) % n, i, :2], tq2_r.at[there, i], vs.at[i, k], vr.at[i, k], (dp, to)
        )

    def far_arrived(i):
        for k in range(3):
            to, _, here = partners[k]
            remote(
                tq.at[(to + 2) % n, i, :2], tq2_r.at[here, i], vs.at[i, k], vr.at[i, k], (dp, to)
            ).wait_recv()

    for i in range(pieces):
        for k in range(3):
            send(near_copy(k, i))
    for i in range(pieces):
        for k in range(3 if i < pieces - 1 else 0):
            send(far_copy(k, i))
    send(far_copy(2, pieces - 1))
    tq_r[c] = tq[me]
    for i in range(pieces):
        tq2_r[c, i] = tq[twin, i, :2]

    loads[6].wait()
    loads[7].wait()
    sg_t[...] = jnp.broadcast_to(sgate[...], (pos, width)).T
    tg_t[...] = jnp.broadcast_to(tgate[...], (pos, width)).T
    lane = lax.broadcasted_iota(jnp.int32, (1, pos), 1)
    frame_live = [(f + first_frame) % n < live_frames for f in range(n)]
    keep = [((lane < live_positions) & frame_live[f]).astype(F32) for f in range(n)]

    def errors(target, gate, h):
        for z in range(outer):
            at = pl.ds(pl.multiple_of((z * 2 + (1 - ox if h == 0 else ox)) * rows, 16), rows)
            column = gate[at, :]
            for f in range(n):
                target[at, f * pos : (f + 1) * pos] = (
                    keep[f] * cot_t[f, h, z].astype(F32) * column
                ).astype(BF16)

    def cot_arrived(h):
        cot_y_arrived(h)
        send(cot_mate(h, 1, c))
        for k in range(2):
            cot_mate(h, k, 1 - c).wait_recv()

    order = list(range(1, outer)) + [0]

    def times(left, right):
        return lax.dot_general(left, right, (((1,), (1,)), ((), ())), preferred_element_type=F32)

    def product(p, source, outs, h):
        main, tail, groups, size = units[p]
        short = rows // groups
        x = 1 - ox if h == 0 else ox
        places = [(oz + j) % outer * 2 + x for j in order]
        strips = [source[pl.ds(pl.multiple_of(d * rows, 16), rows), :] for d in places]
        wide = times(jnp.concatenate(strips, axis=0), outs)
        for i, d in enumerate(places):
            own = wide[i * rows : (i + 1) * rows]
            for k in range(main // 128):
                part[p, d, k * rows : (k + 1) * rows, :] = own[:, k * 128 : (k + 1) * 128].astype(
                    BF16
                )
            if tail:
                edge = [own[k * short : (k + 1) * short, main:] for k in range(groups)]
                if groups * tail < 128:
                    edge.append(jnp.zeros((short, 128 - groups * tail), F32))
                part[p, d, main // 128 * rows : size, :] = jnp.concatenate(edge, axis=1).astype(
                    BF16
                )
            if h == 0:
                send(pair_copy(p, order[i]))

    def pair_copy(p, j):
        z = (oz + j) % outer
        size = units[p][3]
        return remote(
            part.at[p, z * 2 + 1 - ox, :size], xr.at[p, j, :size], xss.at[p, j], xrs.at[p, j],
            (oz * 2 + 1 - ox, me),
        )

    def line_copy(p, j):
        z = (oz + j) % outer
        size = units[p][3]
        return remote(
            zs.at[p, j - 1, :size], zr.at[p, j - 1, :size],
            zss.at[p, j - 1], zrs.at[p, j - 1], (z * 2 + ox, me)
        )

    def line_start(p, j):
        z = (oz + j) % outer
        pair_copy(p, j).wait_recv()
        size = units[p][3]
        zs[p, j - 1, :size, :] = (
            part[p, z * 2 + ox, :size, :].astype(F32) + xr[p, j, :size, :].astype(F32)
        ).astype(BF16)
        send(line_copy(p, j))

    def sum_copy(p):
        size = units[p][3]
        return pltpu.make_async_copy(
            sum_out.at[p, :size], sum_hbm.at[p, :size], out_sem.at[3 + p]
        )

    def line_end(p):
        size = units[p][3]
        pair_copy(p, 0).wait_recv()
        total = part[p, oz * 2 + ox, :size, :].astype(F32) + xr[p, 0, :size, :].astype(F32)
        for j in range(1, outer):
            line_copy(p, j).wait_recv()
            total = total + zr[p, j - 1, :size, :].astype(F32)
        sum_out[p, :size, :] = total
        sum_copy(p).start()

    cot_arrived(0)
    errors(err, sg_t, 0)
    for k in range(3):
        so_arrived(k)
    spatial_rows = jnp.concatenate([so_r[f] for f in range(n)], axis=1)
    product(0, err, spatial_rows, 0)
    errors(err2, tg_t, 0)
    cot_arrived(1)
    errors(err, sg_t, 1)
    product(0, err, spatial_rows, 1)
    errors(err2, tg_t, 1)
    line_start(0, 1)
    loads[3].wait()
    loads[4].wait()
    for b in range(2):
        do_t[b] = (
            jnp.dot(proj[b], err2[...], preferred_element_type=F32).astype(BF16).astype(F32)
        )

    def forward(i):
        kept = []
        for f in range(n):
            for m in range(3):
                tqf[f, i, m] = tq_r[f, i, m].astype(F32)
        for h in range(heads):
            band = slice(h * HD, (h + 1) * HD)
            place = slice(i * half + h * HD, i * half + (h + 1) * HD)
            keys = [tqf[g, i, 1, band, :] for g in range(n)]
            values = [tqf[g, i, 2, band, :] for g in range(n)]
            for f in range(n):
                q = tqf[f, i, 0, band, :]
                row = [
                    jnp.where(
                        frame_live[g], jnp.sum(q * keys[g], axis=0, keepdims=True) * scale, -1e30
                    )
                    for g in range(n)
                ]
                top = functools.reduce(jnp.maximum, row)
                expo = [jnp.exp(value - top) for value in row]
                total = functools.reduce(jnp.add, expo)
                soft = [value / total for value in expo]
                rounded = [value.astype(BF16).astype(F32) for value in soft]
                kept.append((soft, rounded))
                ot[place, f * pos : (f + 1) * pos] = functools.reduce(
                    jnp.add, [rounded[g] * values[g] for g in range(n)]
                ).astype(BF16)
        return kept

    def rows_sent(slopes, weights):
        there = lambda table, a, b: table[(a + 2) % n][(b + 2) % n]
        out = [there(slopes, a, b) for a in range(2) for b in range(n)]
        out += [there(slopes, a, b) for a in range(2, n) for b in range(2)]
        return out + [there(weights, a, b) for a in range(n) for b in range(2)]

    def slopes_copy(i):
        return remote(sl_s.at[i], sl_r.at[i], ls.at[i], lr.at[i], (dp, twin))

    def back_copy(b, i):
        return remote(
            gs.at[1 - c, b, i], gr.at[b, i], us.at[b, i], ur.at[b, i], (dp, mate)
        )

    def add(values):
        return functools.reduce(jnp.add, values)

    def backward(i, kept):
        all_slopes = []
        for h in range(heads):
            band = slice(h * HD, (h + 1) * HD)
            place = slice(i * half + h * HD, i * half + (h + 1) * HD)
            backs = [do_t[0, place, f * pos : (f + 1) * pos] for f in range(n)]
            slopes = []
            for f in range(n):
                soft, _ = kept[h * n + f]
                dw = [
                    jnp.sum(backs[f] * tqf[g, i, 2, band, :], axis=0, keepdims=True)
                    .astype(BF16)
                    .astype(F32)
                    for g in range(n)
                ]
                mean = add([soft[g] * dw[g] for g in range(n)])
                slopes.append([soft[g] * (dw[g] - mean) * scale for g in range(n)])
            all_slopes.append(slopes)
            weights = [kept[h * n + f][1] for f in range(n)]
            out = rows_sent(slopes, weights)
            for k, value in enumerate(out):
                at = h * len(out) + k
                slf[i, at : at + 1, :] = value
        used = heads * len(out)
        if used < slf.shape[1]:
            slf[i, used:, :] = jnp.zeros((slf.shape[1] - used, pos), F32)
        sl_s[i] = slf[i].astype(BF16)
        send(slopes_copy(i))
        for h in range(heads):
            band = slice(h * HD, (h + 1) * HD)
            place = slice(i * half + h * HD, i * half + (h + 1) * HD)
            slopes = all_slopes[h]
            for f in range(2):
                gs[f, 0, i, 0, band, :] = add(
                    [slopes[f][g] * tqf[g, i, 1, band, :] for g in range(n)]
                ).astype(BF16)
                gs[f, 0, i, 1, band, :] = add(
                    [slopes[g][f] * tqf[g, i, 0, band, :] for g in range(n)]
                ).astype(BF16)
                gs[f, 0, i, 2, band, :] = add(
                    [
                        kept[h * n + g][1][f] * do_t[0, place, g * pos : (g + 1) * pos]
                        for g in range(n)
                    ]
                ).astype(BF16)
        send(back_copy(0, i))

    def far_backward(i):
        slopes_copy(i).wait_recv()
        far_arrived(i)
        table = sl_r[i].astype(F32)
        for h in range(heads):
            band = slice(h * HD, (h + 1) * HD)
            place = slice(i * half + h * HD, i * half + (h + 1) * HD)
            at = h * (8 * n - 12)
            row = lambda k: table[at + k : at + k + 1, :]
            for f in range(2):
                along = [row(f * n + g) for g in range(n)]
                down = [row(g * n + f) if g < 2 else row(2 * n + (g - 2) * 2 + f) for g in range(n)]
                mixed = [row(4 * n - 4 + g * 2 + f) for g in range(n)]
                gs[f, 1, i, 0, band, :] = add(
                    [along[g] * tq2_r[g, i, 1, band, :].astype(F32) for g in range(n)]
                ).astype(BF16)
                gs[f, 1, i, 1, band, :] = add(
                    [down[g] * tq2_r[g, i, 0, band, :].astype(F32) for g in range(n)]
                ).astype(BF16)
                gs[f, 1, i, 2, band, :] = add(
                    [mixed[g] * do_t[1, place, g * pos : (g + 1) * pos] for g in range(n)]
                ).astype(BF16)
        send(back_copy(1, i))

    starts = [0]
    for unit in units[1:]:
        starts.append(starts[-1] + unit[0] + unit[1])
    last = pieces

    def lay(refs, b, i):
        for start, source in refs:
            low = pl.multiple_of((start + 2 * b) % n * sl + i * half, 16)
            for m in range(3):
                g_t[m, pl.ds(low, half), :] = source[b, i, m].astype(F32)

    mine, mates = [(me, gs.at[c])], [(mate, gr)]
    waiting = [(0, j) for j in range(2, outer)]

    def lines(number):
        for _ in range(min(number, len(waiting))):
            line_start(*waiting.pop(0))

    for i in range(pieces):
        if i == 0:
            lines(len(waiting) - 1)
        near_arrived(i)
        kept = forward(i)
        outs = ot[starts[i] : starts[i + 1], :]
        for h in range(2):
            product(1 + i, err2, outs, h)
        lines(len(waiting))
        backward(i, kept)
        if i == 0:
            for k in range(2):
                send(far_copy(k, pieces - 1))
        waiting = [(1 + i, j) for j in range(1, outer)]
        if i < pieces - 1:
            lines(1)
        lay(mine, 0, i)
    line_end(0)
    lines(len(waiting) - 1)
    for i in range(pieces - 1):
        far_backward(i)
        lay(mine, 1, i)
    lines(len(waiting))
    for i in range(pieces):
        back_copy(0, i).wait_recv()
        lay(mates, 0, i)
    for i in range(pieces - 1):
        line_end(1 + i)
        back_copy(1, i).wait_recv()
        lay(mates, 1, i)
    far_backward(pieces - 1)
    lay(mine, 1, pieces - 1)
    grad_copies = [
        pltpu.make_async_copy(g_out.at[m], g_hbm.at[m], out_sem.at[m]) for m in range(3)
    ]
    back_copy(1, pieces - 1).wait_recv()
    lay(mates, 1, pieces - 1)
    for m in range(3):
        g_out[m] = g_t[m].T.astype(BF16)
        grad_copies[m].start()
    line_end(last)
    for copy in grad_copies:
        copy.wait()
    for p in range(len(units)):
        sum_copy(p).wait()
    for copy in sent:
        copy.wait_send()


def finish(units, grads, sums, g_out, sp_out, tp_out, held, got, sp, tp, sem):
    rows = sp.shape[0]
    count = grads.shape[0]
    whole = [pltpu.make_async_copy(grads.at[m], held.at[m], sem.at[m]) for m in range(count)]
    gone = [
        pltpu.make_async_copy(held.at[m], g_out.at[m], sem.at[count + m]) for m in range(count)
    ]
    base = 2 * count
    parts = [
        pltpu.make_async_copy(
            sums.at[p, : unit[3]], got.at[p, : unit[3]], sem.at[base + p]
        )
        for p, unit in enumerate(units)
    ]
    base += len(parts)
    for copy in parts[:1] + whole + parts[1:]:
        copy.start()
    outs = [
        pltpu.make_async_copy(sp, sp_out, sem.at[base]),
        pltpu.make_async_copy(tp, tp_out, sem.at[base + 1]),
    ]
    left = 0
    for p, (main, tail, groups, size) in enumerate(units):
        parts[p].wait()
        out = tp if p else sp
        for k in range(main // 128):
            low = left + k * 128
            out[:, low : low + 128] = got[p, k * rows : (k + 1) * rows, :]
        if tail:
            short = rows // groups
            edge = got[p, main // 128 * rows : size, :]
            low = left + main
            for k in range(groups):
                out[k * short : (k + 1) * short, low : low + tail] = edge[
                    :, k * tail : (k + 1) * tail
                ]
        left = left + main + tail if p else 0
        if p == 0:
            outs[0].start()
            for m in range(count):
                whole[m].wait()
                gone[m].start()
    outs[1].start()
    for copy in gone + outs:
        copy.wait()


def unit_of(columns, rows):
    main, tail = columns // 128 * 128, columns % 128
    groups = 1
    if tail:
        groups = max(g for g in range(1, 128 // tail + 1) if rows % (16 * g) == 0)
    return main, tail, groups, main // 128 * rows + (rows // groups if tail else 0)


def kernel_body(
    n, nb, spatial_qkv, temporal_qkv, cotangent, spatial_gate, temporal_gate, temporal_proj, live_counts
):
    pos, width = cotangent.shape[2:]
    sl, rows, outer = width // n, width // nb, nb // 2
    vm, dma = pltpu.VMEM, pltpu.SemaphoreType.DMA
    left = pl.BlockSpec(memory_space=pl.ANY)
    pieces = 2 if sl // HD % 2 == 0 and sl // 2 % 16 == 0 else 1
    half = sl // pieces
    cut = half // 128 * 128
    columns = [cut, sl - cut] if pieces == 2 and cut else [half] * pieces
    units = [unit_of(size, rows) for size in [sl] + columns]
    count, packed = len(units), max(unit[3] for unit in units)
    table = -(-(half // HD * (8 * n - 12)) // 16) * 16
    grads, sums = pl.pallas_call(
        functools.partial(kernel, n, nb, units),
        out_shape=(
            jax.ShapeDtypeStruct((3, pos, width), BF16),
            jax.ShapeDtypeStruct((count, packed, 128), F32),
        ),
        in_specs=[left] * 7,
        out_specs=(left, left),
        scratch_shapes=[
            pltpu.SMEM((1, 2), jnp.int32), vm((1, width), F32), vm((1, width), F32),
            vm((3, pos, width), BF16), vm((count, packed, 128), F32), dma((3 + count,)),
            vm((3, pos, width), BF16), vm((3, pos, width), BF16), vm((pos, width), BF16),
            vm((2, sl, width), BF16), vm((n, 2, outer, rows, pos), BF16),
            vm((width, pos), F32), vm((width, pos), F32),
            vm((width, pos), F32), vm((width, pos), F32), vm((width, pos), F32),
            vm((n, sl, pos), BF16), vm((n, sl, pos), BF16),
            vm((n, pieces, 3, half, pos), BF16), vm((n, pieces, 3, half, pos), BF16),
            vm((n, pieces, 2, half, pos), BF16), vm((n, pieces, 3, half, pos), F32),
            vm((width, n * pos), BF16), vm((width, n * pos), BF16),
            vm((sl, n * pos), BF16), vm((2, sl, n * pos), F32),
            vm((pieces, table, pos), F32), vm((pieces, table, pos), BF16),
            vm((pieces, table, pos), BF16),
            vm((count, nb, packed, 128), BF16), vm((count, outer, packed, 128), BF16),
            vm((count, outer - 1, packed, 128), BF16), vm((count, outer - 1, packed, 128), BF16),
            vm((2, 2, pieces, 3, half, pos), BF16), vm((2, pieces, 3, half, pos), BF16),
            vm((3, width, pos), F32),
            dma((8,)), dma((2,)), dma((2,)), dma((2, 2)), dma((2, 2)),
            dma((3,)), dma((3,)), dma((pieces, 3)), dma((pieces, 3)),
            dma((pieces, 3)), dma((pieces, 3)), dma((pieces,)), dma((pieces,)),
            dma((2, pieces)), dma((2, pieces)),
            dma((count, outer)), dma((count, outer)), dma((count, outer - 1)), dma((count, outer - 1)),
        ],
        compiler_params=pltpu.CompilerParams(
            collective_id=0, has_side_effects=True, vmem_limit_bytes=56 * 1024 * 1024
        ),
    )(
        live_counts, spatial_gate, temporal_gate,
        spatial_qkv.reshape(3, pos, width), temporal_qkv.reshape(3, pos, width),
        cotangent.reshape(pos, width), temporal_proj.reshape(n, sl, width),
    )
    grads, first, second = pl.pallas_call(
        functools.partial(finish, units),
        out_shape=(
            jax.ShapeDtypeStruct((3, pos, width), BF16),
            jax.ShapeDtypeStruct((rows, sl), F32),
            jax.ShapeDtypeStruct((rows, sl), F32),
        ),
        in_specs=[left, left],
        out_specs=(left, left, left),
        scratch_shapes=[
            vm((3, pos, width), BF16),
            vm((count, packed, 128), F32), vm((rows, sl), F32), vm((rows, sl), F32),
            dma((2 * 3 + count + 2,)),
        ],
    )(grads, sums)
    return grads[None, :, None], first.T, second.T


def solution(mesh):
    n, nb = mesh.shape["seq"], mesh.shape["dp"]

    def chosen(*args):
        cot = args[2]
        _, frames, pos, width = cot.shape
        fits = frames == 1 and pos == 128 and width == HEADS * HD and n % 2 == 0 and nb % 2 == 0
        fits = fits and n == 4 and nb > 2 and HEADS % n == 0
        if fits and width // n % 16 == 0 and width // nb % 16 == 0:
            return kernel_body(n, nb, *args)
        return body(*args)

    return jax.shard_map(
        chosen,
        mesh=mesh,
        in_specs=(
            P("dp", None, "seq", None, None),
            P("dp", None, "seq", None, None),
            P("dp", "seq", None, None),
            P("dp", None),
            P("dp", None),
            P(),
            P("dp", None),
        ),
        out_specs=(P("dp", None, "seq", None, None), P("seq", "dp"), P("seq", "dp")),
        check_vma=False,
    )
```

```python
import functools

import jax
import jax.numpy as jnp
from jax import lax
from jax.experimental import pallas as pl
from jax.experimental.pallas import tpu as pltpu
from jax.sharding import PartitionSpec as P

HEADS = 16
HD = 72
MESH = pl.DeviceIdType.MESH
F32 = jnp.float32
BF16 = jnp.bfloat16


def attend(queries, key_block, value_block, key_keep, score_form, mix_form):
    head_split = queries.shape[:-1] + (HEADS, HD)
    q_heads = queries.reshape(head_split)
    k_heads = key_block.reshape(head_split)
    v_heads = value_block.reshape(head_split)
    scores = jnp.einsum(score_form, q_heads, k_heads, preferred_element_type=jnp.float32) * HD ** (
        -0.5
    )
    scores = jnp.where(key_keep[:, None, None, :], scores, -1e30)
    shifted = scores - jnp.max(scores, axis=-1, keepdims=True)
    expo = jnp.exp(shifted)
    attention_weights = (expo / jnp.sum(expo, axis=-1, keepdims=True)).astype(jnp.bfloat16)
    mixed = jnp.einsum(mix_form, attention_weights, v_heads, preferred_element_type=jnp.float32)
    return mixed.reshape(queries.shape)


def body(
    spatial_qkv, temporal_qkv, cotangent, spatial_gate, temporal_gate, temporal_proj, live_counts
):
    spatial = spatial_qkv[0]
    temporal = temporal_qkv[0]
    incoming = cotangent[0]
    frame_count, position_count, width = incoming.shape
    group_size = lax.axis_size("seq")
    member = lax.axis_index("seq")
    live_frames = live_counts[0, 0]
    live_positions = live_counts[0, 1]
    frame_ids = member * frame_count + jnp.arange(frame_count, dtype=jnp.int32)
    position_ids = jnp.arange(position_count, dtype=jnp.int32)
    token_mask = (
        (frame_ids[:, None] < live_frames) & (position_ids[None, :] < live_positions)
    ).astype(jnp.float32)
    flowing = token_mask[:, :, None] * incoming.astype(jnp.float32)
    temporal_error = (flowing * temporal_gate[0]).astype(jnp.bfloat16)
    temporal_back = lax.dot_general(
        temporal_error, temporal_proj, (((2,), (1,)), ((), ())), preferred_element_type=jnp.float32
    ).astype(jnp.bfloat16)
    stacked = jnp.concatenate([temporal, temporal_back[None]], axis=0)
    exchanged = lax.all_to_all(stacked, "seq", split_axis=2, concat_axis=1, tiled=True)
    spatial_keep = position_ids[None, :] < live_positions
    spatial_out = attend(
        spatial[0], spatial[1], spatial[2], spatial_keep, "bqhd,bkhd->bhqk", "bhqk,bkhd->bqhd"
    ).astype(jnp.bfloat16)
    total_frames = exchanged.shape[1]
    slice_positions = exchanged.shape[2]
    temporal_keep = jnp.broadcast_to(
        jnp.arange(total_frames, dtype=jnp.int32)[None, :] < live_frames,
        (slice_positions, total_frames),
    )

    def temporal_attend(queries, key_block, value_block):
        return attend(
            queries, key_block, value_block, temporal_keep, "qbhd,kbhd->bhqk", "bhqk,kbhd->qbhd"
        )

    temporal_result, pullback = jax.vjp(temporal_attend, exchanged[0], exchanged[1], exchanged[2])
    temporal_out = temporal_result.astype(jnp.bfloat16)
    input_grads = jnp.stack(pullback(exchanged[3].astype(jnp.float32)))
    temporal_frames = lax.all_to_all(temporal_out, "seq", split_axis=0, concat_axis=1, tiled=True)
    grads_home = lax.all_to_all(input_grads, "seq", split_axis=1, concat_axis=2, tiled=True)
    tokens = frame_count * position_count
    flat_spatial = spatial_out.reshape(tokens, width)
    flat_temporal = temporal_frames.reshape(tokens, width)
    slice_width = width // group_size
    column_spatial, column_temporal = (
        lax.all_to_all(flat_spatial, "seq", split_axis=1, concat_axis=0, tiled=True),
        lax.all_to_all(flat_temporal, "seq", split_axis=1, concat_axis=0, tiled=True),
    )
    spatial_scale = spatial_gate[0]
    temporal_scale = temporal_gate[0]
    starting = jnp.zeros((slice_width, 2, width), jnp.float32)
    cot_piece = lax.all_gather(incoming.reshape(tokens, width), "seq", axis=0, tiled=True)
    shards = cot_piece.shape[0] // tokens

    def one_block(block, total):
        offset = (block * tokens).astype(jnp.int32)
        rows = lax.dynamic_slice_in_dim(cot_piece, offset, tokens, 0)
        token_index = offset + jnp.arange(tokens, dtype=jnp.int32)
        frame_of = token_index // position_count
        position_of = token_index % position_count
        row_keep = ((frame_of < live_frames) & (position_of < live_positions)).astype(jnp.float32)
        masked_rows = row_keep[:, None] * rows.astype(jnp.float32)
        error_first = (masked_rows * spatial_scale).astype(jnp.bfloat16)
        error_second = (masked_rows * temporal_scale).astype(jnp.bfloat16)
        cols_first = lax.dynamic_slice_in_dim(column_spatial, offset, tokens, 0)
        cols_second = lax.dynamic_slice_in_dim(column_temporal, offset, tokens, 0)
        part_first = lax.dot_general(
            cols_first, error_first, (((0,), (0,)), ((), ())), preferred_element_type=jnp.float32
        )
        part_second = lax.dot_general(
            cols_second, error_second, (((0,), (0,)), ((), ())), preferred_element_type=jnp.float32
        )
        part_first = part_first.astype(jnp.bfloat16).astype(jnp.float32)
        part_second = part_second.astype(jnp.bfloat16).astype(jnp.float32)
        return total + jnp.stack([part_first, part_second], axis=1)

    partial_sum = lax.fori_loop(0, shards, one_block, starting)
    summed = lax.psum_scatter(partial_sum, "dp", scatter_dimension=2, tiled=True)
    return (grads_home[None], summed[:, 0], summed[:, 1])


def kernel(
    n, nb, units, counts_hbm, sgate_hbm, tgate_hbm, sqkv_hbm, tqkv_hbm, cot_hbm, proj_hbm,
    g_out, sum_out,
    counts, sgate, tgate, sqkv, tqkv, cot, proj, cot_t, sg_t, tg_t, q_t, v_t, o_t, so, so_r, tq, tq_r, tq2_r, tqf,
    err, err2, ot, do_t, slf, sl_s, sl_r, part, xr, zs, zr, gs, gr, g_t,
    loc_sem, cs, cr, fs, fr, ss, sr, ts, tr, vs, vr, ls, lr, us, ur, xss, xrs, zss, zrs,
):
    me = lax.axis_index("seq")
    dp = lax.axis_index("dp")
    pos, width = cot.shape
    sl = width // n
    rows = width // nb
    pieces = tq.shape[1]
    half = sl // pieces
    heads = half // HD
    outer = nb // 2
    y, c = me // 2, me % 2
    first_frame = 2 * y
    mate = first_frame + 1 - c
    twin = (me + 2) % n
    cross = (mate + 2) % n
    oz, ox = dp // 2, dp % 2
    scale = HD ** (-0.5)

    loads = [
        pltpu.make_async_copy(cot_hbm, cot, loc_sem.at[0]),
        pltpu.make_async_copy(sqkv_hbm, sqkv, loc_sem.at[1]),
        pltpu.make_async_copy(tqkv_hbm, tqkv, loc_sem.at[2]),
        pltpu.make_async_copy(proj_hbm.at[me], proj.at[0], loc_sem.at[3]),
        pltpu.make_async_copy(proj_hbm.at[twin], proj.at[1], loc_sem.at[4]),
        pltpu.make_async_copy(counts_hbm, counts, loc_sem.at[5]),
        pltpu.make_async_copy(sgate_hbm, sgate, loc_sem.at[6]),
        pltpu.make_async_copy(tgate_hbm, tgate, loc_sem.at[7]),
    ]
    loads[0].start()
    barrier = pltpu.get_barrier_semaphore()
    for j in range(1, n):
        pl.semaphore_signal(barrier, inc=1, device_id=(dp, (me + j) % n), device_id_type=MESH)
    pl.semaphore_signal(barrier, inc=1, device_id=(oz * 2 + 1 - ox, me), device_id_type=MESH)
    for j in range(1, outer):
        pl.semaphore_signal(
            barrier, inc=1, device_id=((oz + j) % outer * 2 + ox, me), device_id_type=MESH
        )

    for load in loads[5:] + loads[1:5]:
        load.start()

    def remote(src, dst, s_sem, r_sem, to):
        return pltpu.make_async_remote_copy(
            src_ref=src, dst_ref=dst, send_sem=s_sem, recv_sem=r_sem, device_id=to,
            device_id_type=MESH,
        )

    def turned(value):
        return value.astype(F32).T

    sent = []

    def send(copy):
        copy.start()
        sent.append(copy)

    partners = [(twin, 2 + c, 2 + c), (cross, 2 + c, 3 - c), (mate, c, 1 - c)]

    loads[0].wait()
    flat = turned(cot[...]).astype(BF16)
    for d in range(nb):
        cot_t[c, (d + ox + 1) % 2, d // 2] = flat[d * rows : (d + 1) * rows, :]
    pl.semaphore_wait(barrier, (n - 1) + 1 + (outer - 1))

    def cot_y(h):
        return remote(cot_t.at[c, h], cot_t.at[2 + c, h], cs.at[h], cr.at[h], (dp, twin))

    def cot_mate(h, k, core):
        slot = 2 * k + core
        return remote(cot_t.at[slot, h], cot_t.at[slot, h], fs.at[k, h], fr.at[k, h], (dp, mate))

    def cot_y_arrived(h):
        remote(cot_t.at[c, h], cot_t.at[2 + c, h], cs.at[h], cr.at[h], (dp, twin)).wait_recv()

    send(cot_y(0))
    for h in range(2):
        send(cot_mate(h, 0, c))

    loads[5].wait()
    live_frames = counts[0, 0]
    live_positions = counts[0, 1]

    loads[1].wait()
    q_t[...] = turned(sqkv[0])
    v_t[...] = turned(sqkv[2])
    key_keep = lax.broadcasted_iota(jnp.int32, (pos, pos), 0) < live_positions
    for h in range(HEADS):
        low = h * HD
        w0 = low // 128 * 128
        w1 = -(-(low + HD) // 128) * 128
        row = lax.broadcasted_iota(jnp.int32, (w1 - w0, pos), 0)
        inside = (row >= low - w0) & (row < low - w0 + HD)
        q_win = jnp.where(inside, q_t[w0:w1, :], 0.0).astype(BF16)
        scores = jnp.dot(sqkv[1, :, w0:w1], q_win, preferred_element_type=F32) * scale
        scores = jnp.where(key_keep, scores, -1e30)
        expo = jnp.exp(scores - jnp.max(scores, axis=0, keepdims=True))
        weights = (expo / jnp.sum(expo, axis=0, keepdims=True)).astype(BF16)
        o_t[low : low + HD, :] = jnp.dot(
            v_t[low : low + HD, :].astype(BF16), weights, preferred_element_type=F32
        )
    for s in range(n):
        so[s] = o_t[s * sl : (s + 1) * sl, :].astype(BF16)

    def so_copy(k):
        to, there, _ = partners[k]
        return remote(so.at[to], so_r.at[there], ss.at[k], sr.at[k], (dp, to))

    def so_arrived(k):
        to, _, here = partners[k]
        remote(so.at[to], so_r.at[here], ss.at[k], sr.at[k], (dp, to)).wait_recv()

    for k in range(3):
        send(so_copy(k))
    send(cot_y(1))
    so_r[c] = so[me]

    loads[2].wait()
    for m in range(3):
        flat = turned(tqkv[m]).astype(BF16)
        for s in range(n):
            for i in range(pieces):
                low = s * sl + i * half
                tq[s, i, m] = flat[low : low + half, :]

    def near_copy(k, i):
        to, there, _ = partners[k]
        return remote(tq.at[to, i], tq_r.at[there, i], ts.at[i, k], tr.at[i, k], (dp, to))

    def near_arrived(i):
        for k in range(3):
            to, _, here = partners[k]
            remote(
                tq.at[to, i], tq_r.at[here, i], ts.at[i, k], tr.at[i, k], (dp, to)
            ).wait_recv()

    def far_copy(k, i):
        to, there, _ = partners[k]
        return remote(
            tq.at[(to + 2) % n, i, :2], tq2_r.at[there, i], vs.at[i, k], vr.at[i, k], (dp, to)
        )

    def far_arrived(i):
        for k in range(3):
            to, _, here = partners[k]
            remote(
                tq.at[(to + 2) % n, i, :2], tq2_r.at[here, i], vs.at[i, k], vr.at[i, k], (dp, to)
            ).wait_recv()

    for i in range(pieces):
        for k in range(3):
            send(near_copy(k, i))
    for i in range(pieces):
        for k in range(3 if i < pieces - 1 else 0):
            send(far_copy(k, i))
    send(far_copy(2, pieces - 1))
    tq_r[c] = tq[me]
    for i in range(pieces):
        tq2_r[c, i] = tq[twin, i, :2]

    loads[6].wait()
    loads[7].wait()
    sg_t[...] = jnp.broadcast_to(sgate[...], (pos, width)).T
    tg_t[...] = jnp.broadcast_to(tgate[...], (pos, width)).T
    lane = lax.broadcasted_iota(jnp.int32, (1, pos), 1)
    frame_live = [(f + first_frame) % n < live_frames for f in range(n)]
    keep = [((lane < live_positions) & frame_live[f]).astype(F32) for f in range(n)]

    def errors(target, gate, h):
        for z in range(outer):
            at = pl.ds(pl.multiple_of((z * 2 + (1 - ox if h == 0 else ox)) * rows, 16), rows)
            column = gate[at, :]
            for f in range(n):
                target[at, f * pos : (f + 1) * pos] = (
                    keep[f] * cot_t[f, h, z].astype(F32) * column
                ).astype(BF16)

    def cot_arrived(h):
        cot_y_arrived(h)
        send(cot_mate(h, 1, c))
        for k in range(2):
            cot_mate(h, k, 1 - c).wait_recv()

    order = list(range(1, outer)) + [0]

    def times(left, right):
        return lax.dot_general(left, right, (((1,), (1,)), ((), ())), preferred_element_type=F32)

    def product(p, source, outs, h):
        main, tail, groups, size = units[p]
        short = rows // groups
        x = 1 - ox if h == 0 else ox
        places = [(oz + j) % outer * 2 + x for j in order]
        strips = [source[pl.ds(pl.multiple_of(d * rows, 16), rows), :] for d in places]
        wide = times(jnp.concatenate(strips, axis=0), outs)
        for i, d in enumerate(places):
            own = wide[i * rows : (i + 1) * rows]
            for k in range(main // 128):
                part[p, d, k * rows : (k + 1) * rows, :] = own[:, k * 128 : (k + 1) * 128].astype(
                    BF16
                )
            if tail:
                edge = [own[k * short : (k + 1) * short, main:] for k in range(groups)]
                if groups * tail < 128:
                    edge.append(jnp.zeros((short, 128 - groups * tail), F32))
                part[p, d, main // 128 * rows : size, :] = jnp.concatenate(edge, axis=1).astype(
                    BF16
                )
            if h == 0:
                send(pair_copy(p, order[i]))

    def pair_copy(p, j):
        z = (oz + j) % outer
        size = units[p][3]
        return remote(
            part.at[p, z * 2 + 1 - ox, :size], xr.at[p, j, :size], xss.at[p, j], xrs.at[p, j],
            (oz * 2 + 1 - ox, me),
        )

    def line_copy(p, j):
        z = (oz + j) % outer
        size = units[p][3]
        return remote(
            zs.at[p, j - 1, :size], zr.at[p, j - 1, :size],
            zss.at[p, j - 1], zrs.at[p, j - 1], (z * 2 + ox, me)
        )

    def line_start(p, j):
        z = (oz + j) % outer
        pair_copy(p, j).wait_recv()
        size = units[p][3]
        zs[p, j - 1, :size, :] = (
            part[p, z * 2 + ox, :size, :].astype(F32) + xr[p, j, :size, :].astype(F32)
        ).astype(BF16)
        send(line_copy(p, j))

    def line_end(p):
        size = units[p][3]
        pair_copy(p, 0).wait_recv()
        total = part[p, oz * 2 + ox, :size, :].astype(F32) + xr[p, 0, :size, :].astype(F32)
        for j in range(1, outer):
            line_copy(p, j).wait_recv()
            total = total + zr[p, j - 1, :size, :].astype(F32)
        sum_out[p, :size, :] = total

    cot_arrived(0)
    errors(err, sg_t, 0)
    for k in range(3):
        so_arrived(k)
    spatial_rows = jnp.concatenate([so_r[f] for f in range(n)], axis=1)
    product(0, err, spatial_rows, 0)
    errors(err2, tg_t, 0)
    cot_arrived(1)
    errors(err, sg_t, 1)
    product(0, err, spatial_rows, 1)
    errors(err2, tg_t, 1)
    line_start(0, 1)
    loads[3].wait()
    loads[4].wait()
    for b in range(2):
        do_t[b] = (
            jnp.dot(proj[b], err2[...], preferred_element_type=F32).astype(BF16).astype(F32)
        )

    def forward(i):
        kept = []
        for f in range(n):
            for m in range(3):
                tqf[f, i, m] = tq_r[f, i, m].astype(F32)
        for h in range(heads):
            band = slice(h * HD, (h + 1) * HD)
            place = slice(i * half + h * HD, i * half + (h + 1) * HD)
            keys = [tqf[g, i, 1, band, :] for g in range(n)]
            values = [tqf[g, i, 2, band, :] for g in range(n)]
            for f in range(n):
                q = tqf[f, i, 0, band, :]
                row = [
                    jnp.where(
                        frame_live[g], jnp.sum(q * keys[g], axis=0, keepdims=True) * scale, -1e30
                    )
                    for g in range(n)
                ]
                top = functools.reduce(jnp.maximum, row)
                expo = [jnp.exp(value - top) for value in row]
                total = functools.reduce(jnp.add, expo)
                soft = [value / total for value in expo]
                rounded = [value.astype(BF16).astype(F32) for value in soft]
                kept.append((soft, rounded))
                ot[place, f * pos : (f + 1) * pos] = functools.reduce(
                    jnp.add, [rounded[g] * values[g] for g in range(n)]
                ).astype(BF16)
        return kept

    def rows_sent(slopes, weights):
        there = lambda table, a, b: table[(a + 2) % n][(b + 2) % n]
        out = [there(slopes, a, b) for a in range(2) for b in range(n)]
        out += [there(slopes, a, b) for a in range(2, n) for b in range(2)]
        return out + [there(weights, a, b) for a in range(n) for b in range(2)]

    def slopes_copy(i):
        return remote(sl_s.at[i], sl_r.at[i], ls.at[i], lr.at[i], (dp, twin))

    def back_copy(b, i):
        return remote(
            gs.at[1 - c, b, i], gr.at[b, i], us.at[b, i], ur.at[b, i], (dp, mate)
        )

    def add(values):
        return functools.reduce(jnp.add, values)

    def backward(i, kept):
        all_slopes = []
        for h in range(heads):
            band = slice(h * HD, (h + 1) * HD)
            place = slice(i * half + h * HD, i * half + (h + 1) * HD)
            backs = [do_t[0, place, f * pos : (f + 1) * pos] for f in range(n)]
            slopes = []
            for f in range(n):
                soft, _ = kept[h * n + f]
                dw = [
                    jnp.sum(backs[f] * tqf[g, i, 2, band, :], axis=0, keepdims=True)
                    .astype(BF16)
                    .astype(F32)
                    for g in range(n)
                ]
                mean = add([soft[g] * dw[g] for g in range(n)])
                slopes.append([soft[g] * (dw[g] - mean) * scale for g in range(n)])
            all_slopes.append(slopes)
            weights = [kept[h * n + f][1] for f in range(n)]
            out = rows_sent(slopes, weights)
            for k, value in enumerate(out):
                at = h * len(out) + k
                slf[i, at : at + 1, :] = value
        used = heads * len(out)
        if used < slf.shape[1]:
            slf[i, used:, :] = jnp.zeros((slf.shape[1] - used, pos), F32)
        sl_s[i] = slf[i].astype(BF16)
        send(slopes_copy(i))
        for h in range(heads):
            band = slice(h * HD, (h + 1) * HD)
            place = slice(i * half + h * HD, i * half + (h + 1) * HD)
            slopes = all_slopes[h]
            for f in range(2):
                gs[f, 0, i, 0, band, :] = add(
                    [slopes[f][g] * tqf[g, i, 1, band, :] for g in range(n)]
                ).astype(BF16)
                gs[f, 0, i, 1, band, :] = add(
                    [slopes[g][f] * tqf[g, i, 0, band, :] for g in range(n)]
                ).astype(BF16)
                gs[f, 0, i, 2, band, :] = add(
                    [
                        kept[h * n + g][1][f] * do_t[0, place, g * pos : (g + 1) * pos]
                        for g in range(n)
                    ]
                ).astype(BF16)
        send(back_copy(0, i))

    def far_backward(i):
        slopes_copy(i).wait_recv()
        far_arrived(i)
        table = sl_r[i].astype(F32)
        for h in range(heads):
            band = slice(h * HD, (h + 1) * HD)
            place = slice(i * half + h * HD, i * half + (h + 1) * HD)
            at = h * (8 * n - 12)
            row = lambda k: table[at + k : at + k + 1, :]
            for f in range(2):
                along = [row(f * n + g) for g in range(n)]
                down = [row(g * n + f) if g < 2 else row(2 * n + (g - 2) * 2 + f) for g in range(n)]
                mixed = [row(4 * n - 4 + g * 2 + f) for g in range(n)]
                gs[f, 1, i, 0, band, :] = add(
                    [along[g] * tq2_r[g, i, 1, band, :].astype(F32) for g in range(n)]
                ).astype(BF16)
                gs[f, 1, i, 1, band, :] = add(
                    [down[g] * tq2_r[g, i, 0, band, :].astype(F32) for g in range(n)]
                ).astype(BF16)
                gs[f, 1, i, 2, band, :] = add(
                    [mixed[g] * do_t[1, place, g * pos : (g + 1) * pos] for g in range(n)]
                ).astype(BF16)
        send(back_copy(1, i))

    starts = [0]
    for unit in units[1:]:
        starts.append(starts[-1] + unit[0] + unit[1])
    last = pieces

    def lay(refs, b, i):
        for start, source in refs:
            low = pl.multiple_of((start + 2 * b) % n * sl + i * half, 16)
            for m in range(3):
                g_t[m, pl.ds(low, half), :] = source[b, i, m].astype(F32)

    mine, mates = [(me, gs.at[c])], [(mate, gr)]
    waiting = [(0, j) for j in range(2, outer)]

    def lines(number):
        for _ in range(min(number, len(waiting))):
            line_start(*waiting.pop(0))

    for i in range(pieces):
        if i == 0:
            lines(len(waiting) - 1)
        near_arrived(i)
        kept = forward(i)
        outs = ot[starts[i] : starts[i + 1], :]
        for h in range(2):
            product(1 + i, err2, outs, h)
        lines(len(waiting))
        backward(i, kept)
        if i == 0:
            for k in range(2):
                send(far_copy(k, pieces - 1))
        waiting = [(1 + i, j) for j in range(1, outer)]
        if i < pieces - 1:
            lines(1)
        lay(mine, 0, i)
    line_end(0)
    lines(len(waiting) - 1)
    for i in range(pieces - 1):
        far_backward(i)
        lay(mine, 1, i)
    lines(len(waiting))
    for i in range(pieces):
        back_copy(0, i).wait_recv()
        lay(mates, 0, i)
    for i in range(pieces - 1):
        line_end(1 + i)
        back_copy(1, i).wait_recv()
        lay(mates, 1, i)
    far_backward(pieces - 1)
    lay(mine, 1, pieces - 1)
    back_copy(1, pieces - 1).wait_recv()
    lay(mates, 1, pieces - 1)
    for m in range(3):
        g_out[m] = g_t[m].T.astype(BF16)
    line_end(last)
    for copy in sent:
        copy.wait_send()


def finish(units, grads, sums, g_out, sp_out, tp_out, sp, tp, sem):
    rows = sp.shape[0]
    count = grads.shape[0]
    gone = [pltpu.make_async_copy(grads.at[m], g_out.at[m], sem.at[m]) for m in range(count)]
    outs = [
        pltpu.make_async_copy(sp, sp_out, sem.at[count]),
        pltpu.make_async_copy(tp, tp_out, sem.at[count + 1]),
    ]
    for copy in gone:
        copy.start()
    left = 0
    for p, (main, tail, groups, size) in enumerate(units):
        out = tp if p else sp
        for k in range(main // 128):
            low = left + k * 128
            out[:, low : low + 128] = sums[p, k * rows : (k + 1) * rows, :]
        if tail:
            short = rows // groups
            edge = sums[p, main // 128 * rows : size, :]
            low = left + main
            for k in range(groups):
                out[k * short : (k + 1) * short, low : low + tail] = edge[
                    :, k * tail : (k + 1) * tail
                ]
        left = left + main + tail if p else 0
        if p == 0:
            outs[0].start()
    outs[1].start()
    for copy in gone + outs:
        copy.wait()


def unit_of(columns, rows):
    main, tail = columns // 128 * 128, columns % 128
    groups = 1
    if tail:
        groups = max(g for g in range(1, 128 // tail + 1) if rows % (16 * g) == 0)
    return main, tail, groups, main // 128 * rows + (rows // groups if tail else 0)


def kernel_body(
    n, nb, spatial_qkv, temporal_qkv, cotangent, spatial_gate, temporal_gate, temporal_proj, live_counts
):
    pos, width = cotangent.shape[2:]
    sl, rows, outer = width // n, width // nb, nb // 2
    vm, dma = pltpu.VMEM, pltpu.SemaphoreType.DMA
    whole = pl.BlockSpec(memory_space=pltpu.VMEM)
    pieces = 2 if sl // HD % 2 == 0 and sl // 2 % 16 == 0 else 1
    half = sl // pieces
    cut = half // 128 * 128
    columns = [cut, sl - cut] if pieces == 2 and cut else [half] * pieces
    units = [unit_of(size, rows) for size in [sl] + columns]
    count, packed = len(units), max(unit[3] for unit in units)
    table = -(-(half // HD * (8 * n - 12)) // 16) * 16
    grads, sums = pl.pallas_call(
        functools.partial(kernel, n, nb, units),
        out_shape=(
            pltpu.VMEM((3, pos, width), BF16),
            pltpu.VMEM((count, packed, 128), F32),
        ),
        in_specs=[pl.BlockSpec(memory_space=pltpu.HBM)] * 7,
        out_specs=(whole, whole),
        scratch_shapes=[
            pltpu.SMEM((1, 2), jnp.int32), vm((1, width), F32), vm((1, width), F32),
            vm((3, pos, width), BF16), vm((3, pos, width), BF16), vm((pos, width), BF16),
            vm((2, sl, width), BF16), vm((n, 2, outer, rows, pos), BF16),
            vm((width, pos), F32), vm((width, pos), F32),
            vm((width, pos), F32), vm((width, pos), F32), vm((width, pos), F32),
            vm((n, sl, pos), BF16), vm((n, sl, pos), BF16),
            vm((n, pieces, 3, half, pos), BF16), vm((n, pieces, 3, half, pos), BF16),
            vm((n, pieces, 2, half, pos), BF16), vm((n, pieces, 3, half, pos), F32),
            vm((width, n * pos), BF16), vm((width, n * pos), BF16),
            vm((sl, n * pos), BF16), vm((2, sl, n * pos), F32),
            vm((pieces, table, pos), F32), vm((pieces, table, pos), BF16),
            vm((pieces, table, pos), BF16),
            vm((count, nb, packed, 128), BF16), vm((count, outer, packed, 128), BF16),
            vm((count, outer - 1, packed, 128), BF16), vm((count, outer - 1, packed, 128), BF16),
            vm((2, 2, pieces, 3, half, pos), BF16), vm((2, pieces, 3, half, pos), BF16),
            vm((3, width, pos), F32),
            dma((8,)), dma((2,)), dma((2,)), dma((2, 2)), dma((2, 2)),
            dma((3,)), dma((3,)), dma((pieces, 3)), dma((pieces, 3)),
            dma((pieces, 3)), dma((pieces, 3)), dma((pieces,)), dma((pieces,)),
            dma((2, pieces)), dma((2, pieces)),
            dma((count, outer)), dma((count, outer)), dma((count, outer - 1)), dma((count, outer - 1)),
        ],
        compiler_params=pltpu.CompilerParams(
            collective_id=0, has_side_effects=True, vmem_limit_bytes=60 * 1024 * 1024
        ),
    )(
        live_counts, spatial_gate, temporal_gate,
        spatial_qkv.reshape(3, pos, width), temporal_qkv.reshape(3, pos, width),
        cotangent.reshape(pos, width), temporal_proj.reshape(n, sl, width),
    )
    grads, first, second = pl.pallas_call(
        functools.partial(finish, units),
        out_shape=(
            jax.ShapeDtypeStruct((3, pos, width), BF16),
            jax.ShapeDtypeStruct((rows, sl), F32),
            jax.ShapeDtypeStruct((rows, sl), F32),
        ),
        in_specs=[whole, whole],
        out_specs=tuple(pl.BlockSpec(memory_space=pltpu.HBM) for _ in range(3)),
        scratch_shapes=[vm((rows, sl), F32), vm((rows, sl), F32), dma((3 + 2,))],
        compiler_params=pltpu.CompilerParams(vmem_limit_bytes=4 * 1024 * 1024),
    )(grads, sums)
    return grads[None, :, None], first.T, second.T


def solution(mesh):
    n, nb = mesh.shape["seq"], mesh.shape["dp"]

    def chosen(*args):
        cot = args[2]
        _, frames, pos, width = cot.shape
        fits = frames == 1 and pos == 128 and width == HEADS * HD and n % 2 == 0 and nb % 2 == 0
        fits = fits and n == 4 and nb > 2 and HEADS % n == 0
        if fits and width // n % 16 == 0 and width // nb % 16 == 0:
            return kernel_body(n, nb, *args)
        return body(*args)

    return jax.shard_map(
        chosen,
        mesh=mesh,
        in_specs=(
            P("dp", None, "seq", None, None),
            P("dp", None, "seq", None, None),
            P("dp", "seq", None, None),
            P("dp", None),
            P("dp", None),
            P(),
            P("dp", None),
        ),
        out_specs=(P("dp", None, "seq", None, None), P("seq", "dp"), P("seq", "dp")),
        check_vma=False,
    )
```

```python
import functools

import jax
import jax.numpy as jnp
from jax import lax
from jax.experimental import pallas as pl
from jax.experimental.pallas import tpu as pltpu
from jax.sharding import PartitionSpec as P

HEADS = 16
HD = 72
MESH = pl.DeviceIdType.MESH
F32 = jnp.float32
BF16 = jnp.bfloat16


def attend(queries, key_block, value_block, key_keep, score_form, mix_form):
    head_split = queries.shape[:-1] + (HEADS, HD)
    q_heads = queries.reshape(head_split)
    k_heads = key_block.reshape(head_split)
    v_heads = value_block.reshape(head_split)
    scores = jnp.einsum(score_form, q_heads, k_heads, preferred_element_type=jnp.float32) * HD ** (
        -0.5
    )
    scores = jnp.where(key_keep[:, None, None, :], scores, -1e30)
    shifted = scores - jnp.max(scores, axis=-1, keepdims=True)
    expo = jnp.exp(shifted)
    attention_weights = (expo / jnp.sum(expo, axis=-1, keepdims=True)).astype(jnp.bfloat16)
    mixed = jnp.einsum(mix_form, attention_weights, v_heads, preferred_element_type=jnp.float32)
    return mixed.reshape(queries.shape)


def body(
    spatial_qkv, temporal_qkv, cotangent, spatial_gate, temporal_gate, temporal_proj, live_counts
):
    spatial = spatial_qkv[0]
    temporal = temporal_qkv[0]
    incoming = cotangent[0]
    frame_count, position_count, width = incoming.shape
    group_size = lax.axis_size("seq")
    member = lax.axis_index("seq")
    live_frames = live_counts[0, 0]
    live_positions = live_counts[0, 1]
    frame_ids = member * frame_count + jnp.arange(frame_count, dtype=jnp.int32)
    position_ids = jnp.arange(position_count, dtype=jnp.int32)
    token_mask = (
        (frame_ids[:, None] < live_frames) & (position_ids[None, :] < live_positions)
    ).astype(jnp.float32)
    flowing = token_mask[:, :, None] * incoming.astype(jnp.float32)
    temporal_error = (flowing * temporal_gate[0]).astype(jnp.bfloat16)
    temporal_back = lax.dot_general(
        temporal_error, temporal_proj, (((2,), (1,)), ((), ())), preferred_element_type=jnp.float32
    ).astype(jnp.bfloat16)
    stacked = jnp.concatenate([temporal, temporal_back[None]], axis=0)
    exchanged = lax.all_to_all(stacked, "seq", split_axis=2, concat_axis=1, tiled=True)
    spatial_keep = position_ids[None, :] < live_positions
    spatial_out = attend(
        spatial[0], spatial[1], spatial[2], spatial_keep, "bqhd,bkhd->bhqk", "bhqk,bkhd->bqhd"
    ).astype(jnp.bfloat16)
    total_frames = exchanged.shape[1]
    slice_positions = exchanged.shape[2]
    temporal_keep = jnp.broadcast_to(
        jnp.arange(total_frames, dtype=jnp.int32)[None, :] < live_frames,
        (slice_positions, total_frames),
    )

    def temporal_attend(queries, key_block, value_block):
        return attend(
            queries, key_block, value_block, temporal_keep, "qbhd,kbhd->bhqk", "bhqk,kbhd->qbhd"
        )

    temporal_result, pullback = jax.vjp(temporal_attend, exchanged[0], exchanged[1], exchanged[2])
    temporal_out = temporal_result.astype(jnp.bfloat16)
    input_grads = jnp.stack(pullback(exchanged[3].astype(jnp.float32)))
    temporal_frames = lax.all_to_all(temporal_out, "seq", split_axis=0, concat_axis=1, tiled=True)
    grads_home = lax.all_to_all(input_grads, "seq", split_axis=1, concat_axis=2, tiled=True)
    tokens = frame_count * position_count
    flat_spatial = spatial_out.reshape(tokens, width)
    flat_temporal = temporal_frames.reshape(tokens, width)
    slice_width = width // group_size
    column_spatial, column_temporal = (
        lax.all_to_all(flat_spatial, "seq", split_axis=1, concat_axis=0, tiled=True),
        lax.all_to_all(flat_temporal, "seq", split_axis=1, concat_axis=0, tiled=True),
    )
    spatial_scale = spatial_gate[0]
    temporal_scale = temporal_gate[0]
    starting = jnp.zeros((slice_width, 2, width), jnp.float32)
    cot_piece = lax.all_gather(incoming.reshape(tokens, width), "seq", axis=0, tiled=True)
    shards = cot_piece.shape[0] // tokens

    def one_block(block, total):
        offset = (block * tokens).astype(jnp.int32)
        rows = lax.dynamic_slice_in_dim(cot_piece, offset, tokens, 0)
        token_index = offset + jnp.arange(tokens, dtype=jnp.int32)
        frame_of = token_index // position_count
        position_of = token_index % position_count
        row_keep = ((frame_of < live_frames) & (position_of < live_positions)).astype(jnp.float32)
        masked_rows = row_keep[:, None] * rows.astype(jnp.float32)
        error_first = (masked_rows * spatial_scale).astype(jnp.bfloat16)
        error_second = (masked_rows * temporal_scale).astype(jnp.bfloat16)
        cols_first = lax.dynamic_slice_in_dim(column_spatial, offset, tokens, 0)
        cols_second = lax.dynamic_slice_in_dim(column_temporal, offset, tokens, 0)
        part_first = lax.dot_general(
            cols_first, error_first, (((0,), (0,)), ((), ())), preferred_element_type=jnp.float32
        )
        part_second = lax.dot_general(
            cols_second, error_second, (((0,), (0,)), ((), ())), preferred_element_type=jnp.float32
        )
        part_first = part_first.astype(jnp.bfloat16).astype(jnp.float32)
        part_second = part_second.astype(jnp.bfloat16).astype(jnp.float32)
        return total + jnp.stack([part_first, part_second], axis=1)

    partial_sum = lax.fori_loop(0, shards, one_block, starting)
    summed = lax.psum_scatter(partial_sum, "dp", scatter_dimension=2, tiled=True)
    return (grads_home[None], summed[:, 0], summed[:, 1])


def kernel(
    n, nb, units, counts_hbm, sgate_hbm, tgate_hbm, sqkv_hbm, tqkv_hbm, cot_hbm, proj_hbm,
    g_out, sum_out,
    counts, sgate, tgate, sqkv, tqkv, cot, proj, cot_t, sg_t, tg_t, q_t, v_t, o_t, so, so_r, tq, tq_r, tq2_r, tqf,
    err, err2, ot, do_t, slf, sl_s, sl_r, part, xr, zs, zr, gs, gr, g_t,
    loc_sem, cs, cr, fs, fr, ss, sr, ts, tr, vs, vr, ls, lr, us, ur, xss, xrs, zss, zrs,
):
    me = lax.axis_index("seq")
    dp = lax.axis_index("dp")
    pos, width = cot.shape
    sl = width // n
    rows = width // nb
    pieces = tq.shape[1]
    half = sl // pieces
    heads = half // HD
    outer = nb // 2
    y, c = me // 2, me % 2
    first_frame = 2 * y
    mate = first_frame + 1 - c
    twin = (me + 2) % n
    cross = (mate + 2) % n
    oz, ox = dp // 2, dp % 2
    scale = HD ** (-0.5)

    loads = [
        pltpu.make_async_copy(cot_hbm, cot, loc_sem.at[0]),
        pltpu.make_async_copy(sqkv_hbm, sqkv, loc_sem.at[1]),
        pltpu.make_async_copy(tqkv_hbm, tqkv, loc_sem.at[2]),
        pltpu.make_async_copy(proj_hbm.at[me], proj.at[0], loc_sem.at[3]),
        pltpu.make_async_copy(proj_hbm.at[twin], proj.at[1], loc_sem.at[4]),
        pltpu.make_async_copy(counts_hbm, counts, loc_sem.at[5]),
        pltpu.make_async_copy(sgate_hbm, sgate, loc_sem.at[6]),
        pltpu.make_async_copy(tgate_hbm, tgate, loc_sem.at[7]),
    ]
    loads[0].start()
    barrier = pltpu.get_barrier_semaphore()
    for j in range(1, n):
        pl.semaphore_signal(barrier, inc=1, device_id=(dp, (me + j) % n), device_id_type=MESH)
    pl.semaphore_signal(barrier, inc=1, device_id=(oz * 2 + 1 - ox, me), device_id_type=MESH)
    for j in range(1, outer):
        pl.semaphore_signal(
            barrier, inc=1, device_id=((oz + j) % outer * 2 + ox, me), device_id_type=MESH
        )

    for load in loads[5:] + loads[1:5]:
        load.start()

    def remote(src, dst, s_sem, r_sem, to):
        return pltpu.make_async_remote_copy(
            src_ref=src, dst_ref=dst, send_sem=s_sem, recv_sem=r_sem, device_id=to,
            device_id_type=MESH,
        )

    def turned(value):
        return value.astype(F32).T

    sent = []

    def send(copy):
        copy.start()
        sent.append(copy)

    partners = [(twin, 2 + c, 2 + c), (cross, 2 + c, 3 - c), (mate, c, 1 - c)]

    cuts = [(0, 0, outer), (1, 0, outer - 1), (1, outer - 1, outer)]
    loads[0].wait()
    flat = turned(cot[...]).astype(BF16)
    for d in range(nb):
        cot_t[c, (d + ox + 1) % 2, (d // 2 + outer - oz - 1) % outer] = flat[
            d * rows : (d + 1) * rows, :
        ]
    pl.semaphore_wait(barrier, (n - 1) + 1 + (outer - 1))

    def cot_part(slot, t):
        h, low, high = cuts[t]
        return cot_t.at[slot, h, low:high]

    def cot_y(t):
        return remote(cot_part(c, t), cot_part(2 + c, t), cs.at[t], cr.at[t], (dp, twin))

    def cot_mate(t, k, core):
        slot = 2 * k + core
        return remote(cot_part(slot, t), cot_part(slot, t), fs.at[k, t], fr.at[k, t], (dp, mate))

    send(cot_y(0))
    for t in range(3):
        send(cot_mate(t, 0, c))

    loads[5].wait()
    live_frames = counts[0, 0]
    live_positions = counts[0, 1]

    loads[1].wait()
    q_t[...] = turned(sqkv[0])
    v_t[...] = turned(sqkv[2])
    key_keep = lax.broadcasted_iota(jnp.int32, (pos, pos), 0) < live_positions
    for h in range(HEADS):
        low = h * HD
        w0 = low // 128 * 128
        w1 = -(-(low + HD) // 128) * 128
        row = lax.broadcasted_iota(jnp.int32, (w1 - w0, pos), 0)
        inside = (row >= low - w0) & (row < low - w0 + HD)
        q_win = jnp.where(inside, q_t[w0:w1, :], 0.0).astype(BF16)
        scores = jnp.dot(sqkv[1, :, w0:w1], q_win, preferred_element_type=F32) * scale
        scores = jnp.where(key_keep, scores, -1e30)
        expo = jnp.exp(scores - jnp.max(scores, axis=0, keepdims=True))
        weights = (expo / jnp.sum(expo, axis=0, keepdims=True)).astype(BF16)
        o_t[low : low + HD, :] = jnp.dot(
            v_t[low : low + HD, :].astype(BF16), weights, preferred_element_type=F32
        )
    for s in range(n):
        so[s] = o_t[s * sl : (s + 1) * sl, :].astype(BF16)

    def so_copy(k):
        to, there, _ = partners[k]
        return remote(so.at[to], so_r.at[there], ss.at[k], sr.at[k], (dp, to))

    def so_arrived(k):
        to, _, here = partners[k]
        remote(so.at[to], so_r.at[here], ss.at[k], sr.at[k], (dp, to)).wait_recv()

    for k in range(3):
        send(so_copy(k))
    send(cot_y(1))
    so_r[c] = so[me]

    loads[2].wait()
    for m in range(3):
        flat = turned(tqkv[m]).astype(BF16)
        for s in range(n):
            for i in range(pieces):
                low = s * sl + i * half
                tq[s, i, m] = flat[low : low + half, :]

    def near_copy(k, i):
        to, there, _ = partners[k]
        return remote(tq.at[to, i], tq_r.at[there, i], ts.at[i, k], tr.at[i, k], (dp, to))

    def near_arrived(i):
        for k in range(3):
            to, _, here = partners[k]
            remote(
                tq.at[to, i], tq_r.at[here, i], ts.at[i, k], tr.at[i, k], (dp, to)
            ).wait_recv()

    def far_copy(k, i):
        to, there, _ = partners[k]
        return remote(
            tq.at[(to + 2) % n, i, :2], tq2_r.at[there, i], vs.at[i, k], vr.at[i, k], (dp, to)
        )

    def far_arrived(i):
        for k in range(3):
            to, _, here = partners[k]
            remote(
                tq.at[(to + 2) % n, i, :2], tq2_r.at[here, i], vs.at[i, k], vr.at[i, k], (dp, to)
            ).wait_recv()

    for i in range(pieces):
        for k in range(3):
            send(near_copy(k, i))
    send(cot_y(2))
    for i in range(pieces):
        for k in range(3 if i < pieces - 1 else 0):
            send(far_copy(k, i))
    send(far_copy(2, pieces - 1))
    tq_r[c] = tq[me]
    for i in range(pieces):
        tq2_r[c, i] = tq[twin, i, :2]

    loads[6].wait()
    loads[7].wait()
    sg_t[...] = jnp.broadcast_to(sgate[...], (pos, width)).T
    tg_t[...] = jnp.broadcast_to(tgate[...], (pos, width)).T
    lane = lax.broadcasted_iota(jnp.int32, (1, pos), 1)
    frame_live = [(f + first_frame) % n < live_frames for f in range(n)]
    keep = [((lane < live_positions) & frame_live[f]).astype(F32) for f in range(n)]

    def errors(target, gate, t):
        h, low, high = cuts[t]
        for q in range(low, high):
            d = (oz + 1 + q) % outer * 2 + (1 - ox if h == 0 else ox)
            at = pl.ds(pl.multiple_of(d * rows, 16), rows)
            column = gate[at, :]
            for f in range(n):
                target[at, f * pos : (f + 1) * pos] = (
                    keep[f] * cot_t[f, h, q].astype(F32) * column
                ).astype(BF16)

    def cot_arrived(t):
        cot_y(t).wait_recv()
        send(cot_mate(t, 1, c))
        for k in range(2):
            cot_mate(t, k, 1 - c).wait_recv()

    order = list(range(1, outer)) + [0]

    def times(left, right):
        return lax.dot_general(left, right, (((1,), (1,)), ((), ())), preferred_element_type=F32)

    def product(p, source, outs, t):
        h, low, high = cuts[t]
        main, tail, groups, size = units[p]
        short = rows // groups
        x = 1 - ox if h == 0 else ox
        places = [(oz + j) % outer * 2 + x for j in order[low:high]]
        strips = [source[pl.ds(pl.multiple_of(d * rows, 16), rows), :] for d in places]
        wide = times(jnp.concatenate(strips, axis=0), outs)
        for i, d in enumerate(places):
            own = wide[i * rows : (i + 1) * rows]
            for k in range(main // 128):
                part[p, d, k * rows : (k + 1) * rows, :] = own[:, k * 128 : (k + 1) * 128].astype(
                    BF16
                )
            if tail:
                edge = [own[k * short : (k + 1) * short, main:] for k in range(groups)]
                if groups * tail < 128:
                    edge.append(jnp.zeros((short, 128 - groups * tail), F32))
                part[p, d, main // 128 * rows : size, :] = jnp.concatenate(edge, axis=1).astype(
                    BF16
                )
            if h == 0:
                send(pair_copy(p, order[i]))

    def pair_copy(p, j):
        z = (oz + j) % outer
        size = units[p][3]
        return remote(
            part.at[p, z * 2 + 1 - ox, :size], xr.at[p, j, :size], xss.at[p, j], xrs.at[p, j],
            (oz * 2 + 1 - ox, me),
        )

    def line_copy(p, j):
        z = (oz + j) % outer
        size = units[p][3]
        return remote(
            zs.at[p, j - 1, :size], zr.at[p, j - 1, :size],
            zss.at[p, j - 1], zrs.at[p, j - 1], (z * 2 + ox, me)
        )

    def line_start(p, j):
        z = (oz + j) % outer
        pair_copy(p, j).wait_recv()
        size = units[p][3]
        zs[p, j - 1, :size, :] = (
            part[p, z * 2 + ox, :size, :].astype(F32) + xr[p, j, :size, :].astype(F32)
        ).astype(BF16)
        send(line_copy(p, j))

    def line_end(p):
        size = units[p][3]
        pair_copy(p, 0).wait_recv()
        total = part[p, oz * 2 + ox, :size, :].astype(F32) + xr[p, 0, :size, :].astype(F32)
        for j in range(1, outer):
            line_copy(p, j).wait_recv()
            total = total + zr[p, j - 1, :size, :].astype(F32)
        sum_out[p, :size, :] = total

    cot_arrived(0)
    errors(err, sg_t, 0)
    for k in range(3):
        so_arrived(k)
    spatial_rows = jnp.concatenate([so_r[f] for f in range(n)], axis=1)
    product(0, err, spatial_rows, 0)
    errors(err2, tg_t, 0)
    cot_arrived(1)
    errors(err, sg_t, 1)
    product(0, err, spatial_rows, 1)
    errors(err2, tg_t, 1)
    line_start(0, 1)

    def forward(i):
        kept = []
        for f in range(n):
            for m in range(3):
                tqf[f, i, m] = tq_r[f, i, m].astype(F32)
        for h in range(heads):
            band = slice(h * HD, (h + 1) * HD)
            place = slice(i * half + h * HD, i * half + (h + 1) * HD)
            keys = [tqf[g, i, 1, band, :] for g in range(n)]
            values = [tqf[g, i, 2, band, :] for g in range(n)]
            for f in range(n):
                q = tqf[f, i, 0, band, :]
                row = [
                    jnp.where(
                        frame_live[g], jnp.sum(q * keys[g], axis=0, keepdims=True) * scale, -1e30
                    )
                    for g in range(n)
                ]
                top = functools.reduce(jnp.maximum, row)
                expo = [jnp.exp(value - top) for value in row]
                total = functools.reduce(jnp.add, expo)
                soft = [value / total for value in expo]
                rounded = [value.astype(BF16).astype(F32) for value in soft]
                kept.append((soft, rounded))
                ot[place, f * pos : (f + 1) * pos] = functools.reduce(
                    jnp.add, [rounded[g] * values[g] for g in range(n)]
                ).astype(BF16)
        return kept

    def rows_sent(slopes, weights):
        there = lambda table, a, b: table[(a + 2) % n][(b + 2) % n]
        out = [there(slopes, a, b) for a in range(2) for b in range(n)]
        out += [there(slopes, a, b) for a in range(2, n) for b in range(2)]
        return out + [there(weights, a, b) for a in range(n) for b in range(2)]

    def slopes_copy(i):
        return remote(sl_s.at[i], sl_r.at[i], ls.at[i], lr.at[i], (dp, twin))

    def back_copy(b, i):
        return remote(
            gs.at[1 - c, b, i], gr.at[b, i], us.at[b, i], ur.at[b, i], (dp, mate)
        )

    def add(values):
        return functools.reduce(jnp.add, values)

    def backward(i, kept):
        all_slopes = []
        for h in range(heads):
            band = slice(h * HD, (h + 1) * HD)
            place = slice(i * half + h * HD, i * half + (h + 1) * HD)
            backs = [do_t[0, place, f * pos : (f + 1) * pos] for f in range(n)]
            slopes = []
            for f in range(n):
                soft, _ = kept[h * n + f]
                dw = [
                    jnp.sum(backs[f] * tqf[g, i, 2, band, :], axis=0, keepdims=True)
                    .astype(BF16)
                    .astype(F32)
                    for g in range(n)
                ]
                mean = add([soft[g] * dw[g] for g in range(n)])
                slopes.append([soft[g] * (dw[g] - mean) * scale for g in range(n)])
            all_slopes.append(slopes)
            weights = [kept[h * n + f][1] for f in range(n)]
            out = rows_sent(slopes, weights)
            for k, value in enumerate(out):
                at = h * len(out) + k
                slf[i, at : at + 1, :] = value
        used = heads * len(out)
        if used < slf.shape[1]:
            slf[i, used:, :] = jnp.zeros((slf.shape[1] - used, pos), F32)
        sl_s[i] = slf[i].astype(BF16)
        send(slopes_copy(i))
        for h in range(heads):
            band = slice(h * HD, (h + 1) * HD)
            place = slice(i * half + h * HD, i * half + (h + 1) * HD)
            slopes = all_slopes[h]
            for f in range(2):
                gs[f, 0, i, 0, band, :] = add(
                    [slopes[f][g] * tqf[g, i, 1, band, :] for g in range(n)]
                ).astype(BF16)
                gs[f, 0, i, 1, band, :] = add(
                    [slopes[g][f] * tqf[g, i, 0, band, :] for g in range(n)]
                ).astype(BF16)
                gs[f, 0, i, 2, band, :] = add(
                    [
                        kept[h * n + g][1][f] * do_t[0, place, g * pos : (g + 1) * pos]
                        for g in range(n)
                    ]
                ).astype(BF16)
        send(back_copy(0, i))

    def far_backward(i):
        slopes_copy(i).wait_recv()
        far_arrived(i)
        table = sl_r[i].astype(F32)
        for h in range(heads):
            band = slice(h * HD, (h + 1) * HD)
            place = slice(i * half + h * HD, i * half + (h + 1) * HD)
            at = h * (8 * n - 12)
            row = lambda k: table[at + k : at + k + 1, :]
            for f in range(2):
                along = [row(f * n + g) for g in range(n)]
                down = [row(g * n + f) if g < 2 else row(2 * n + (g - 2) * 2 + f) for g in range(n)]
                mixed = [row(4 * n - 4 + g * 2 + f) for g in range(n)]
                gs[f, 1, i, 0, band, :] = add(
                    [along[g] * tq2_r[g, i, 1, band, :].astype(F32) for g in range(n)]
                ).astype(BF16)
                gs[f, 1, i, 1, band, :] = add(
                    [down[g] * tq2_r[g, i, 0, band, :].astype(F32) for g in range(n)]
                ).astype(BF16)
                gs[f, 1, i, 2, band, :] = add(
                    [mixed[g] * do_t[1, place, g * pos : (g + 1) * pos] for g in range(n)]
                ).astype(BF16)
        send(back_copy(1, i))

    starts = [0]
    for unit in units[1:]:
        starts.append(starts[-1] + unit[0] + unit[1])
    last = pieces

    def lay(refs, b, i):
        for start, source in refs:
            low = pl.multiple_of((start + 2 * b) % n * sl + i * half, 16)
            for m in range(3):
                g_t[m, pl.ds(low, half), :] = source[b, i, m].astype(F32)

    mine, mates = [(me, gs.at[c])], [(mate, gr)]
    waiting = [(0, j) for j in range(2, outer)]

    def lines(number):
        for _ in range(min(number, len(waiting))):
            line_start(*waiting.pop(0))

    kept = []
    for i in range(pieces):
        lines(len(waiting) - 1 if i == 0 else 1)
        near_arrived(i)
        kept.append(forward(i))
        outs = ot[starts[i] : starts[i + 1], :]
        for t in range(2):
            product(1 + i, err2, outs, t)
        lines(len(waiting))
        waiting = [(1 + i, j) for j in range(1, outer)]
    cot_arrived(2)
    errors(err2, tg_t, 2)
    loads[3].wait()
    loads[4].wait()
    for b in range(2):
        do_t[b] = (
            jnp.dot(proj[b], err2[...], preferred_element_type=F32).astype(BF16).astype(F32)
        )
    for i in range(pieces):
        backward(i, kept[i])
        if i == 0:
            for k in range(2):
                send(far_copy(k, pieces - 1))
        lines(1)
        lay(mine, 0, i)
    errors(err, sg_t, 2)
    product(0, err, spatial_rows, 2)
    for i in range(pieces):
        product(1 + i, err2, ot[starts[i] : starts[i + 1], :], 2)
    line_end(0)
    lines(len(waiting) - 1)
    lines(len(waiting))
    for i in range(pieces - 1):
        far_backward(i)
        lay(mine, 1, i)
    for i in range(pieces):
        back_copy(0, i).wait_recv()
        lay(mates, 0, i)
    for i in range(pieces - 1):
        line_end(1 + i)
        back_copy(1, i).wait_recv()
        lay(mates, 1, i)
    far_backward(pieces - 1)
    lay(mine, 1, pieces - 1)
    back_copy(1, pieces - 1).wait_recv()
    lay(mates, 1, pieces - 1)
    for m in range(3):
        g_out[m] = g_t[m].T.astype(BF16)
    line_end(last)
    for copy in sent:
        copy.wait_send()


def finish(units, grads, sums, g_out, sp_out, tp_out, sp, tp, sem):
    rows = sp.shape[0]
    count = grads.shape[0]
    gone = [pltpu.make_async_copy(grads.at[m], g_out.at[m], sem.at[m]) for m in range(count)]
    outs = [
        pltpu.make_async_copy(sp, sp_out, sem.at[count]),
        pltpu.make_async_copy(tp, tp_out, sem.at[count + 1]),
    ]
    for copy in gone:
        copy.start()
    left = 0
    for p, (main, tail, groups, size) in enumerate(units):
        out = tp if p else sp
        for k in range(main // 128):
            low = left + k * 128
            out[:, low : low + 128] = sums[p, k * rows : (k + 1) * rows, :]
        if tail:
            short = rows // groups
            edge = sums[p, main // 128 * rows : size, :]
            low = left + main
            for k in range(groups):
                out[k * short : (k + 1) * short, low : low + tail] = edge[
                    :, k * tail : (k + 1) * tail
                ]
        left = left + main + tail if p else 0
        if p == 0:
            outs[0].start()
    outs[1].start()
    for copy in gone + outs:
        copy.wait()


def unit_of(columns, rows):
    main, tail = columns // 128 * 128, columns % 128
    groups = 1
    if tail:
        groups = max(g for g in range(1, 128 // tail + 1) if rows % (16 * g) == 0)
    return main, tail, groups, main // 128 * rows + (rows // groups if tail else 0)


def kernel_body(
    n, nb, spatial_qkv, temporal_qkv, cotangent, spatial_gate, temporal_gate, temporal_proj, live_counts
):
    pos, width = cotangent.shape[2:]
    sl, rows, outer = width // n, width // nb, nb // 2
    vm, dma = pltpu.VMEM, pltpu.SemaphoreType.DMA
    whole = pl.BlockSpec(memory_space=pltpu.VMEM)
    pieces = 2 if sl // HD % 2 == 0 and sl // 2 % 16 == 0 else 1
    half = sl // pieces
    cut = half // 128 * 128
    columns = [cut, sl - cut] if pieces == 2 and cut else [half] * pieces
    units = [unit_of(size, rows) for size in [sl] + columns]
    count, packed = len(units), max(unit[3] for unit in units)
    table = -(-(half // HD * (8 * n - 12)) // 16) * 16
    grads, sums = pl.pallas_call(
        functools.partial(kernel, n, nb, units),
        out_shape=(
            pltpu.VMEM((3, pos, width), BF16),
            pltpu.VMEM((count, packed, 128), F32),
        ),
        in_specs=[pl.BlockSpec(memory_space=pltpu.HBM)] * 7,
        out_specs=(whole, whole),
        scratch_shapes=[
            pltpu.SMEM((1, 2), jnp.int32), vm((1, width), F32), vm((1, width), F32),
            vm((3, pos, width), BF16), vm((3, pos, width), BF16), vm((pos, width), BF16),
            vm((2, sl, width), BF16), vm((n, 2, outer, rows, pos), BF16),
            vm((width, pos), F32), vm((width, pos), F32),
            vm((width, pos), F32), vm((width, pos), F32), vm((width, pos), F32),
            vm((n, sl, pos), BF16), vm((n, sl, pos), BF16),
            vm((n, pieces, 3, half, pos), BF16), vm((n, pieces, 3, half, pos), BF16),
            vm((n, pieces, 2, half, pos), BF16), vm((n, pieces, 3, half, pos), F32),
            vm((width, n * pos), BF16), vm((width, n * pos), BF16),
            vm((sl, n * pos), BF16), vm((2, sl, n * pos), F32),
            vm((pieces, table, pos), F32), vm((pieces, table, pos), BF16),
            vm((pieces, table, pos), BF16),
            vm((count, nb, packed, 128), BF16), vm((count, outer, packed, 128), BF16),
            vm((count, outer - 1, packed, 128), BF16), vm((count, outer - 1, packed, 128), BF16),
            vm((2, 2, pieces, 3, half, pos), BF16), vm((2, pieces, 3, half, pos), BF16),
            vm((3, width, pos), F32),
            dma((8,)), dma((3,)), dma((3,)), dma((2, 3)), dma((2, 3)),
            dma((3,)), dma((3,)), dma((pieces, 3)), dma((pieces, 3)),
            dma((pieces, 3)), dma((pieces, 3)), dma((pieces,)), dma((pieces,)),
            dma((2, pieces)), dma((2, pieces)),
            dma((count, outer)), dma((count, outer)), dma((count, outer - 1)), dma((count, outer - 1)),
        ],
        compiler_params=pltpu.CompilerParams(
            collective_id=0, has_side_effects=True, vmem_limit_bytes=60 * 1024 * 1024
        ),
    )(
        live_counts, spatial_gate, temporal_gate,
        spatial_qkv.reshape(3, pos, width), temporal_qkv.reshape(3, pos, width),
        cotangent.reshape(pos, width), temporal_proj.reshape(n, sl, width),
    )
    grads, first, second = pl.pallas_call(
        functools.partial(finish, units),
        out_shape=(
            jax.ShapeDtypeStruct((3, pos, width), BF16),
            jax.ShapeDtypeStruct((rows, sl), F32),
            jax.ShapeDtypeStruct((rows, sl), F32),
        ),
        in_specs=[whole, whole],
        out_specs=tuple(pl.BlockSpec(memory_space=pltpu.HBM) for _ in range(3)),
        scratch_shapes=[vm((rows, sl), F32), vm((rows, sl), F32), dma((3 + 2,))],
        compiler_params=pltpu.CompilerParams(vmem_limit_bytes=4 * 1024 * 1024),
    )(grads, sums)
    return grads[None, :, None], first.T, second.T


def solution(mesh):
    n, nb = mesh.shape["seq"], mesh.shape["dp"]

    def chosen(*args):
        cot = args[2]
        _, frames, pos, width = cot.shape
        fits = frames == 1 and pos == 128 and width == HEADS * HD and n % 2 == 0 and nb % 2 == 0
        fits = fits and n == 4 and nb > 2 and HEADS % n == 0
        if fits and width // n % 16 == 0 and width // nb % 16 == 0:
            return kernel_body(n, nb, *args)
        return body(*args)

    return jax.shard_map(
        chosen,
        mesh=mesh,
        in_specs=(
            P("dp", None, "seq", None, None),
            P("dp", None, "seq", None, None),
            P("dp", "seq", None, None),
            P("dp", None),
            P("dp", None),
            P(),
            P("dp", None),
        ),
        out_specs=(P("dp", None, "seq", None, None), P("seq", "dp"), P("seq", "dp")),
        check_vma=False,
    )
```

```python
import functools

import jax
import jax.numpy as jnp
from jax import lax
from jax.experimental import pallas as pl
from jax.experimental.pallas import tpu as pltpu
from jax.sharding import PartitionSpec as P

HEADS = 16
HD = 72
MESH = pl.DeviceIdType.MESH
F32 = jnp.float32
BF16 = jnp.bfloat16


def attend(queries, key_block, value_block, key_keep, score_form, mix_form):
    head_split = queries.shape[:-1] + (HEADS, HD)
    q_heads = queries.reshape(head_split)
    k_heads = key_block.reshape(head_split)
    v_heads = value_block.reshape(head_split)
    scores = jnp.einsum(score_form, q_heads, k_heads, preferred_element_type=jnp.float32) * HD ** (
        -0.5
    )
    scores = jnp.where(key_keep[:, None, None, :], scores, -1e30)
    shifted = scores - jnp.max(scores, axis=-1, keepdims=True)
    expo = jnp.exp(shifted)
    attention_weights = (expo / jnp.sum(expo, axis=-1, keepdims=True)).astype(jnp.bfloat16)
    mixed = jnp.einsum(mix_form, attention_weights, v_heads, preferred_element_type=jnp.float32)
    return mixed.reshape(queries.shape)


def body(
    spatial_qkv, temporal_qkv, cotangent, spatial_gate, temporal_gate, temporal_proj, live_counts
):
    spatial = spatial_qkv[0]
    temporal = temporal_qkv[0]
    incoming = cotangent[0]
    frame_count, position_count, width = incoming.shape
    group_size = lax.axis_size("seq")
    member = lax.axis_index("seq")
    live_frames = live_counts[0, 0]
    live_positions = live_counts[0, 1]
    frame_ids = member * frame_count + jnp.arange(frame_count, dtype=jnp.int32)
    position_ids = jnp.arange(position_count, dtype=jnp.int32)
    token_mask = (
        (frame_ids[:, None] < live_frames) & (position_ids[None, :] < live_positions)
    ).astype(jnp.float32)
    flowing = token_mask[:, :, None] * incoming.astype(jnp.float32)
    temporal_error = (flowing * temporal_gate[0]).astype(jnp.bfloat16)
    temporal_back = lax.dot_general(
        temporal_error, temporal_proj, (((2,), (1,)), ((), ())), preferred_element_type=jnp.float32
    ).astype(jnp.bfloat16)
    stacked = jnp.concatenate([temporal, temporal_back[None]], axis=0)
    exchanged = lax.all_to_all(stacked, "seq", split_axis=2, concat_axis=1, tiled=True)
    spatial_keep = position_ids[None, :] < live_positions
    spatial_out = attend(
        spatial[0], spatial[1], spatial[2], spatial_keep, "bqhd,bkhd->bhqk", "bhqk,bkhd->bqhd"
    ).astype(jnp.bfloat16)
    total_frames = exchanged.shape[1]
    slice_positions = exchanged.shape[2]
    temporal_keep = jnp.broadcast_to(
        jnp.arange(total_frames, dtype=jnp.int32)[None, :] < live_frames,
        (slice_positions, total_frames),
    )

    def temporal_attend(queries, key_block, value_block):
        return attend(
            queries, key_block, value_block, temporal_keep, "qbhd,kbhd->bhqk", "bhqk,kbhd->qbhd"
        )

    temporal_result, pullback = jax.vjp(temporal_attend, exchanged[0], exchanged[1], exchanged[2])
    temporal_out = temporal_result.astype(jnp.bfloat16)
    input_grads = jnp.stack(pullback(exchanged[3].astype(jnp.float32)))
    temporal_frames = lax.all_to_all(temporal_out, "seq", split_axis=0, concat_axis=1, tiled=True)
    grads_home = lax.all_to_all(input_grads, "seq", split_axis=1, concat_axis=2, tiled=True)
    tokens = frame_count * position_count
    flat_spatial = spatial_out.reshape(tokens, width)
    flat_temporal = temporal_frames.reshape(tokens, width)
    slice_width = width // group_size
    column_spatial, column_temporal = (
        lax.all_to_all(flat_spatial, "seq", split_axis=1, concat_axis=0, tiled=True),
        lax.all_to_all(flat_temporal, "seq", split_axis=1, concat_axis=0, tiled=True),
    )
    spatial_scale = spatial_gate[0]
    temporal_scale = temporal_gate[0]
    starting = jnp.zeros((slice_width, 2, width), jnp.float32)
    cot_piece = lax.all_gather(incoming.reshape(tokens, width), "seq", axis=0, tiled=True)
    shards = cot_piece.shape[0] // tokens

    def one_block(block, total):
        offset = (block * tokens).astype(jnp.int32)
        rows = lax.dynamic_slice_in_dim(cot_piece, offset, tokens, 0)
        token_index = offset + jnp.arange(tokens, dtype=jnp.int32)
        frame_of = token_index // position_count
        position_of = token_index % position_count
        row_keep = ((frame_of < live_frames) & (position_of < live_positions)).astype(jnp.float32)
        masked_rows = row_keep[:, None] * rows.astype(jnp.float32)
        error_first = (masked_rows * spatial_scale).astype(jnp.bfloat16)
        error_second = (masked_rows * temporal_scale).astype(jnp.bfloat16)
        cols_first = lax.dynamic_slice_in_dim(column_spatial, offset, tokens, 0)
        cols_second = lax.dynamic_slice_in_dim(column_temporal, offset, tokens, 0)
        part_first = lax.dot_general(
            cols_first, error_first, (((0,), (0,)), ((), ())), preferred_element_type=jnp.float32
        )
        part_second = lax.dot_general(
            cols_second, error_second, (((0,), (0,)), ((), ())), preferred_element_type=jnp.float32
        )
        part_first = part_first.astype(jnp.bfloat16).astype(jnp.float32)
        part_second = part_second.astype(jnp.bfloat16).astype(jnp.float32)
        return total + jnp.stack([part_first, part_second], axis=1)

    partial_sum = lax.fori_loop(0, shards, one_block, starting)
    summed = lax.psum_scatter(partial_sum, "dp", scatter_dimension=2, tiled=True)
    return (grads_home[None], summed[:, 0], summed[:, 1])


def kernel(
    n, nb, units, counts_hbm, sgate_hbm, tgate_hbm, sqkv_hbm, tqkv_hbm, cot_hbm, proj_hbm,
    g_out, sum_out,
    counts, sgate, tgate, sqkv, tqkv, cot, proj, cot_t, sg_t, tg_t, q_t, v_t, o_t, so, so_r, tq, tq_r, tq2_r, tqf,
    err, err2, ot, do_t, slf, sl_s, sl_r, part, xr, zs, zr, gs, gr, g_t,
    loc_sem, cs, cr, fs, fr, ss, sr, ts, tr, vs, vr, ls, lr, us, ur, xss, xrs, zss, zrs,
):
    me = lax.axis_index("seq")
    dp = lax.axis_index("dp")
    pos, width = cot.shape
    sl = width // n
    rows = width // nb
    pieces = tq.shape[1]
    half = sl // pieces
    heads = half // HD
    outer = nb // 2
    y, c = me // 2, me % 2
    first_frame = 2 * y
    mate = first_frame + 1 - c
    twin = (me + 2) % n
    cross = (mate + 2) % n
    oz, ox = dp // 2, dp % 2
    scale = HD ** (-0.5)

    loads = [
        pltpu.make_async_copy(cot_hbm, cot, loc_sem.at[0]),
        pltpu.make_async_copy(sqkv_hbm, sqkv, loc_sem.at[1]),
        pltpu.make_async_copy(tqkv_hbm, tqkv, loc_sem.at[2]),
        pltpu.make_async_copy(proj_hbm.at[me], proj.at[0], loc_sem.at[3]),
        pltpu.make_async_copy(proj_hbm.at[twin], proj.at[1], loc_sem.at[4]),
        pltpu.make_async_copy(counts_hbm, counts, loc_sem.at[5]),
        pltpu.make_async_copy(sgate_hbm, sgate, loc_sem.at[6]),
        pltpu.make_async_copy(tgate_hbm, tgate, loc_sem.at[7]),
    ]
    loads[0].start()
    barrier = pltpu.get_barrier_semaphore()
    for j in range(1, n):
        pl.semaphore_signal(barrier, inc=1, device_id=(dp, (me + j) % n), device_id_type=MESH)
    pl.semaphore_signal(barrier, inc=1, device_id=(oz * 2 + 1 - ox, me), device_id_type=MESH)
    for j in range(1, outer):
        pl.semaphore_signal(
            barrier, inc=1, device_id=((oz + j) % outer * 2 + ox, me), device_id_type=MESH
        )

    for load in loads[5:] + loads[1:5]:
        load.start()

    def remote(src, dst, s_sem, r_sem, to):
        return pltpu.make_async_remote_copy(
            src_ref=src, dst_ref=dst, send_sem=s_sem, recv_sem=r_sem, device_id=to,
            device_id_type=MESH,
        )

    def turned(value):
        return value.astype(F32).T

    sent = []

    def send(copy):
        copy.start()
        sent.append(copy)

    partners = [(twin, 2 + c, 2 + c), (cross, 2 + c, 3 - c), (mate, c, 1 - c)]

    cuts = [(0, 0, outer), (1, 0, outer - 1), (1, outer - 1, outer)]
    loads[0].wait()
    flat = turned(cot[...]).astype(BF16)
    for d in range(nb):
        cot_t[c, (d + ox + 1) % 2, (d // 2 + outer - oz - 1) % outer] = flat[
            d * rows : (d + 1) * rows, :
        ]
    pl.semaphore_wait(barrier, (n - 1) + 1 + (outer - 1))

    def cot_part(slot, t):
        h, low, high = cuts[t]
        return cot_t.at[slot, h, low:high]

    def cot_y(t):
        return remote(cot_part(c, t), cot_part(2 + c, t), cs.at[t], cr.at[t], (dp, twin))

    def cot_mate(t, k, core):
        slot = 2 * k + core
        return remote(cot_part(slot, t), cot_part(slot, t), fs.at[k, t], fr.at[k, t], (dp, mate))

    send(cot_y(0))
    for t in range(3):
        send(cot_mate(t, 0, c))

    loads[5].wait()
    live_frames = counts[0, 0]
    live_positions = counts[0, 1]

    loads[1].wait()
    q_t[...] = turned(sqkv[0])
    v_t[...] = turned(sqkv[2])
    key_keep = lax.broadcasted_iota(jnp.int32, (pos, pos), 0) < live_positions
    for h in range(HEADS):
        low = h * HD
        w0 = low // 128 * 128
        w1 = -(-(low + HD) // 128) * 128
        row = lax.broadcasted_iota(jnp.int32, (w1 - w0, pos), 0)
        inside = (row >= low - w0) & (row < low - w0 + HD)
        q_win = jnp.where(inside, q_t[w0:w1, :], 0.0).astype(BF16)
        scores = jnp.dot(sqkv[1, :, w0:w1], q_win, preferred_element_type=F32) * scale
        scores = jnp.where(key_keep, scores, -1e30)
        expo = jnp.exp(scores - jnp.max(scores, axis=0, keepdims=True))
        weights = (expo / jnp.sum(expo, axis=0, keepdims=True)).astype(BF16)
        o_t[low : low + HD, :] = jnp.dot(
            v_t[low : low + HD, :].astype(BF16), weights, preferred_element_type=F32
        )
    for s in range(n):
        so[s] = o_t[s * sl : (s + 1) * sl, :].astype(BF16)

    ns = len(units) - pieces
    spans = [0]
    for unit in units[:ns]:
        spans.append(spans[-1] + unit[0] + unit[1])

    def so_copy(k, u):
        to, there, _ = partners[k]
        rows_of = slice(spans[u], spans[u + 1])
        return remote(
            so.at[to, rows_of], so_r.at[there, rows_of], ss.at[u, k], sr.at[u, k], (dp, to)
        )

    def so_arrived(k, u):
        to, _, here = partners[k]
        rows_of = slice(spans[u], spans[u + 1])
        remote(
            so.at[to, rows_of], so_r.at[here, rows_of], ss.at[u, k], sr.at[u, k], (dp, to)
        ).wait_recv()

    for u in range(ns):
        for k in range(3):
            send(so_copy(k, u))
        if u == 0:
            send(cot_y(1))
    so_r[c] = so[me]

    loads[2].wait()
    for m in range(3):
        flat = turned(tqkv[m]).astype(BF16)
        for s in range(n):
            for i in range(pieces):
                low = s * sl + i * half
                tq[s, i, m] = flat[low : low + half, :]

    def near_copy(k, i):
        to, there, _ = partners[k]
        return remote(tq.at[to, i], tq_r.at[there, i], ts.at[i, k], tr.at[i, k], (dp, to))

    def near_arrived(i):
        for k in range(3):
            to, _, here = partners[k]
            remote(
                tq.at[to, i], tq_r.at[here, i], ts.at[i, k], tr.at[i, k], (dp, to)
            ).wait_recv()

    def far_copy(k, i):
        to, there, _ = partners[k]
        return remote(
            tq.at[(to + 2) % n, i, :2], tq2_r.at[there, i], vs.at[i, k], vr.at[i, k], (dp, to)
        )

    def far_arrived(i):
        for k in range(3):
            to, _, here = partners[k]
            remote(
                tq.at[(to + 2) % n, i, :2], tq2_r.at[here, i], vs.at[i, k], vr.at[i, k], (dp, to)
            ).wait_recv()

    for i in range(pieces):
        for k in range(3):
            send(near_copy(k, i))
    send(cot_y(2))
    for i in range(pieces):
        for k in range(3 if i < pieces - 1 else 0):
            send(far_copy(k, i))
    send(far_copy(2, pieces - 1))
    tq_r[c] = tq[me]
    for i in range(pieces):
        tq2_r[c, i] = tq[twin, i, :2]

    loads[6].wait()
    loads[7].wait()
    sg_t[...] = jnp.broadcast_to(sgate[...], (pos, width)).T
    tg_t[...] = jnp.broadcast_to(tgate[...], (pos, width)).T
    lane = lax.broadcasted_iota(jnp.int32, (1, pos), 1)
    frame_live = [(f + first_frame) % n < live_frames for f in range(n)]
    keep = [((lane < live_positions) & frame_live[f]).astype(F32) for f in range(n)]

    def errors(target, gate, t):
        h, low, high = cuts[t]
        for q in range(low, high):
            d = (oz + 1 + q) % outer * 2 + (1 - ox if h == 0 else ox)
            at = pl.ds(pl.multiple_of(d * rows, 16), rows)
            column = gate[at, :]
            for f in range(n):
                target[at, f * pos : (f + 1) * pos] = (
                    keep[f] * cot_t[f, h, q].astype(F32) * column
                ).astype(BF16)

    def cot_arrived(t):
        cot_y(t).wait_recv()
        send(cot_mate(t, 1, c))
        for k in range(2):
            cot_mate(t, k, 1 - c).wait_recv()

    order = list(range(1, outer)) + [0]

    def times(left, right):
        return lax.dot_general(left, right, (((1,), (1,)), ((), ())), preferred_element_type=F32)

    def product(p, source, outs, t):
        h, low, high = cuts[t]
        main, tail, groups, size = units[p]
        short = rows // groups
        x = 1 - ox if h == 0 else ox
        places = [(oz + j) % outer * 2 + x for j in order[low:high]]
        strips = [source[pl.ds(pl.multiple_of(d * rows, 16), rows), :] for d in places]
        wide = times(jnp.concatenate(strips, axis=0), outs)
        for i, d in enumerate(places):
            own = wide[i * rows : (i + 1) * rows]
            for k in range(main // 128):
                part[p, d, k * rows : (k + 1) * rows, :] = own[:, k * 128 : (k + 1) * 128].astype(
                    BF16
                )
            if tail:
                edge = [own[k * short : (k + 1) * short, main:] for k in range(groups)]
                if groups * tail < 128:
                    edge.append(jnp.zeros((short, 128 - groups * tail), F32))
                part[p, d, main // 128 * rows : size, :] = jnp.concatenate(edge, axis=1).astype(
                    BF16
                )
            if h == 0:
                send(pair_copy(p, order[i]))

    def pair_copy(p, j):
        z = (oz + j) % outer
        size = units[p][3]
        return remote(
            part.at[p, z * 2 + 1 - ox, :size], xr.at[p, j, :size], xss.at[p, j], xrs.at[p, j],
            (oz * 2 + 1 - ox, me),
        )

    def line_copy(p, j):
        z = (oz + j) % outer
        size = units[p][3]
        return remote(
            zs.at[p, j - 1, :size], zr.at[p, j - 1, :size],
            zss.at[p, j - 1], zrs.at[p, j - 1], (z * 2 + ox, me)
        )

    def line_start(p, j):
        z = (oz + j) % outer
        pair_copy(p, j).wait_recv()
        size = units[p][3]
        zs[p, j - 1, :size, :] = (
            part[p, z * 2 + ox, :size, :].astype(F32) + xr[p, j, :size, :].astype(F32)
        ).astype(BF16)
        send(line_copy(p, j))

    def line_end(p):
        size = units[p][3]
        pair_copy(p, 0).wait_recv()
        total = part[p, oz * 2 + ox, :size, :].astype(F32) + xr[p, 0, :size, :].astype(F32)
        for j in range(1, outer):
            line_copy(p, j).wait_recv()
            total = total + zr[p, j - 1, :size, :].astype(F32)
        sum_out[p, :size, :] = total

    cot_arrived(0)
    errors(err, sg_t, 0)

    def spatial_rows(u):
        return jnp.concatenate([so_r[f, spans[u] : spans[u + 1]] for f in range(n)], axis=1)

    for k in range(3):
        so_arrived(k, 0)
    product(0, err, spatial_rows(0), 0)
    errors(err2, tg_t, 0)
    cot_arrived(1)
    errors(err, sg_t, 1)
    product(0, err, spatial_rows(0), 1)
    line_start(0, 1)
    for u in range(1, ns):
        for k in range(3):
            so_arrived(k, u)
        for t in range(2):
            product(u, err, spatial_rows(u), t)
    errors(err2, tg_t, 1)

    def forward(i):
        kept = []
        for f in range(n):
            for m in range(3):
                tqf[f, i, m] = tq_r[f, i, m].astype(F32)
        for h in range(heads):
            band = slice(h * HD, (h + 1) * HD)
            place = slice(i * half + h * HD, i * half + (h + 1) * HD)
            keys = [tqf[g, i, 1, band, :] for g in range(n)]
            values = [tqf[g, i, 2, band, :] for g in range(n)]
            for f in range(n):
                q = tqf[f, i, 0, band, :]
                row = [
                    jnp.where(
                        frame_live[g], jnp.sum(q * keys[g], axis=0, keepdims=True) * scale, -1e30
                    )
                    for g in range(n)
                ]
                top = functools.reduce(jnp.maximum, row)
                expo = [jnp.exp(value - top) for value in row]
                total = functools.reduce(jnp.add, expo)
                soft = [value / total for value in expo]
                rounded = [value.astype(BF16).astype(F32) for value in soft]
                kept.append((soft, rounded))
                ot[place, f * pos : (f + 1) * pos] = functools.reduce(
                    jnp.add, [rounded[g] * values[g] for g in range(n)]
                ).astype(BF16)
        return kept

    def rows_sent(slopes, weights):
        there = lambda table, a, b: table[(a + 2) % n][(b + 2) % n]
        out = [there(slopes, a, b) for a in range(2) for b in range(n)]
        out += [there(slopes, a, b) for a in range(2, n) for b in range(2)]
        return out + [there(weights, a, b) for a in range(n) for b in range(2)]

    def slopes_copy(i):
        return remote(sl_s.at[i], sl_r.at[i], ls.at[i], lr.at[i], (dp, twin))

    def back_copy(b, i):
        return remote(
            gs.at[1 - c, b, i], gr.at[b, i], us.at[b, i], ur.at[b, i], (dp, mate)
        )

    def add(values):
        return functools.reduce(jnp.add, values)

    def backward(i, kept):
        all_slopes = []
        for h in range(heads):
            band = slice(h * HD, (h + 1) * HD)
            place = slice(i * half + h * HD, i * half + (h + 1) * HD)
            backs = [do_t[0, place, f * pos : (f + 1) * pos] for f in range(n)]
            slopes = []
            for f in range(n):
                soft, _ = kept[h * n + f]
                dw = [
                    jnp.sum(backs[f] * tqf[g, i, 2, band, :], axis=0, keepdims=True)
                    .astype(BF16)
                    .astype(F32)
                    for g in range(n)
                ]
                mean = add([soft[g] * dw[g] for g in range(n)])
                slopes.append([soft[g] * (dw[g] - mean) * scale for g in range(n)])
            all_slopes.append(slopes)
            weights = [kept[h * n + f][1] for f in range(n)]
            out = rows_sent(slopes, weights)
            for k, value in enumerate(out):
                at = h * len(out) + k
                slf[i, at : at + 1, :] = value
        used = heads * len(out)
        if used < slf.shape[1]:
            slf[i, used:, :] = jnp.zeros((slf.shape[1] - used, pos), F32)
        sl_s[i] = slf[i].astype(BF16)
        send(slopes_copy(i))
        for h in range(heads):
            band = slice(h * HD, (h + 1) * HD)
            place = slice(i * half + h * HD, i * half + (h + 1) * HD)
            slopes = all_slopes[h]
            for f in range(2):
                gs[f, 0, i, 0, band, :] = add(
                    [slopes[f][g] * tqf[g, i, 1, band, :] for g in range(n)]
                ).astype(BF16)
                gs[f, 0, i, 1, band, :] = add(
                    [slopes[g][f] * tqf[g, i, 0, band, :] for g in range(n)]
                ).astype(BF16)
                gs[f, 0, i, 2, band, :] = add(
                    [
                        kept[h * n + g][1][f] * do_t[0, place, g * pos : (g + 1) * pos]
                        for g in range(n)
                    ]
                ).astype(BF16)
        send(back_copy(0, i))

    def far_backward(i):
        slopes_copy(i).wait_recv()
        far_arrived(i)
        table = sl_r[i].astype(F32)
        for h in range(heads):
            band = slice(h * HD, (h + 1) * HD)
            place = slice(i * half + h * HD, i * half + (h + 1) * HD)
            at = h * (8 * n - 12)
            row = lambda k: table[at + k : at + k + 1, :]
            for f in range(2):
                along = [row(f * n + g) for g in range(n)]
                down = [row(g * n + f) if g < 2 else row(2 * n + (g - 2) * 2 + f) for g in range(n)]
                mixed = [row(4 * n - 4 + g * 2 + f) for g in range(n)]
                gs[f, 1, i, 0, band, :] = add(
                    [along[g] * tq2_r[g, i, 1, band, :].astype(F32) for g in range(n)]
                ).astype(BF16)
                gs[f, 1, i, 1, band, :] = add(
                    [down[g] * tq2_r[g, i, 0, band, :].astype(F32) for g in range(n)]
                ).astype(BF16)
                gs[f, 1, i, 2, band, :] = add(
                    [mixed[g] * do_t[1, place, g * pos : (g + 1) * pos] for g in range(n)]
                ).astype(BF16)
        send(back_copy(1, i))

    starts = [0]
    for unit in units[ns:]:
        starts.append(starts[-1] + unit[0] + unit[1])
    last = ns + pieces - 1

    def lay(refs, b, i):
        for start, source in refs:
            low = pl.multiple_of((start + 2 * b) % n * sl + i * half, 16)
            for m in range(3):
                g_t[m, pl.ds(low, half), :] = source[b, i, m].astype(F32)

    mine, mates = [(me, gs.at[c])], [(mate, gr)]
    waiting = [(0, j) for j in range(2, outer)]
    waiting += [(u, j) for u in range(1, ns) for j in range(1, outer)]

    def lines(number):
        for _ in range(min(number, len(waiting))):
            line_start(*waiting.pop(0))

    kept = []
    for i in range(pieces):
        lines(len(waiting) - 1 if i == 0 else 1)
        near_arrived(i)
        kept.append(forward(i))
        outs = ot[starts[i] : starts[i + 1], :]
        for t in range(2):
            product(ns + i, err2, outs, t)
        lines(len(waiting))
        waiting = [(ns + i, j) for j in range(1, outer)]
    cot_arrived(2)
    errors(err2, tg_t, 2)
    loads[3].wait()
    loads[4].wait()
    for b in range(2):
        do_t[b] = (
            jnp.dot(proj[b], err2[...], preferred_element_type=F32).astype(BF16).astype(F32)
        )
    for i in range(pieces):
        backward(i, kept[i])
        if i == 0:
            for k in range(2):
                send(far_copy(k, pieces - 1))
        lines(1)
        lay(mine, 0, i)
    errors(err, sg_t, 2)
    for u in range(ns):
        product(u, err, spatial_rows(u), 2)
    for i in range(pieces):
        product(ns + i, err2, ot[starts[i] : starts[i + 1], :], 2)
    for u in range(ns):
        line_end(u)
    lines(len(waiting) - 1)
    lines(len(waiting))
    for i in range(pieces - 1):
        far_backward(i)
        lay(mine, 1, i)
    for i in range(pieces):
        back_copy(0, i).wait_recv()
        lay(mates, 0, i)
    for i in range(pieces - 1):
        line_end(ns + i)
        back_copy(1, i).wait_recv()
        lay(mates, 1, i)
    far_backward(pieces - 1)
    lay(mine, 1, pieces - 1)
    back_copy(1, pieces - 1).wait_recv()
    lay(mates, 1, pieces - 1)
    for m in range(3):
        g_out[m] = g_t[m].T.astype(BF16)
    line_end(last)
    for copy in sent:
        copy.wait_send()


def finish(units, grads, sums, g_out, sp_out, tp_out, sp, tp, sem):
    rows = sp.shape[0]
    count = grads.shape[0]
    gone = [pltpu.make_async_copy(grads.at[m], g_out.at[m], sem.at[m]) for m in range(count)]
    outs = [
        pltpu.make_async_copy(sp, sp_out, sem.at[count]),
        pltpu.make_async_copy(tp, tp_out, sem.at[count + 1]),
    ]
    for copy in gone:
        copy.start()
    left = 0
    for p, (main, tail, groups, size) in enumerate(units):
        out = tp if p >= len(units) // 2 else sp
        for k in range(main // 128):
            low = left + k * 128
            out[:, low : low + 128] = sums[p, k * rows : (k + 1) * rows, :]
        if tail:
            short = rows // groups
            edge = sums[p, main // 128 * rows : size, :]
            low = left + main
            for k in range(groups):
                out[k * short : (k + 1) * short, low : low + tail] = edge[
                    :, k * tail : (k + 1) * tail
                ]
        left += main + tail
        if p == len(units) // 2 - 1:
            outs[0].start()
            left = 0
    outs[1].start()
    for copy in gone + outs:
        copy.wait()


def unit_of(columns, rows):
    main, tail = columns // 128 * 128, columns % 128
    groups = 1
    if tail:
        groups = max(g for g in range(1, 128 // tail + 1) if rows % (16 * g) == 0)
    return main, tail, groups, main // 128 * rows + (rows // groups if tail else 0)


def kernel_body(
    n, nb, spatial_qkv, temporal_qkv, cotangent, spatial_gate, temporal_gate, temporal_proj, live_counts
):
    pos, width = cotangent.shape[2:]
    sl, rows, outer = width // n, width // nb, nb // 2
    vm, dma = pltpu.VMEM, pltpu.SemaphoreType.DMA
    whole = pl.BlockSpec(memory_space=pltpu.VMEM)
    pieces = 2 if sl // HD % 2 == 0 and sl // 2 % 16 == 0 else 1
    half = sl // pieces
    cut = half // 128 * 128
    columns = [cut, sl - cut] if pieces == 2 and cut else [half] * pieces
    units = [unit_of(size, rows) for size in columns + columns]
    count, packed = len(units), max(unit[3] for unit in units)
    table = -(-(half // HD * (8 * n - 12)) // 16) * 16
    grads, sums = pl.pallas_call(
        functools.partial(kernel, n, nb, units),
        out_shape=(
            pltpu.VMEM((3, pos, width), BF16),
            pltpu.VMEM((count, packed, 128), F32),
        ),
        in_specs=[pl.BlockSpec(memory_space=pltpu.HBM)] * 7,
        out_specs=(whole, whole),
        scratch_shapes=[
            pltpu.SMEM((1, 2), jnp.int32), vm((1, width), F32), vm((1, width), F32),
            vm((3, pos, width), BF16), vm((3, pos, width), BF16), vm((pos, width), BF16),
            vm((2, sl, width), BF16), vm((n, 2, outer, rows, pos), BF16),
            vm((width, pos), F32), vm((width, pos), F32),
            vm((width, pos), F32), vm((width, pos), F32), vm((width, pos), F32),
            vm((n, sl, pos), BF16), vm((n, sl, pos), BF16),
            vm((n, pieces, 3, half, pos), BF16), vm((n, pieces, 3, half, pos), BF16),
            vm((n, pieces, 2, half, pos), BF16), vm((n, pieces, 3, half, pos), F32),
            vm((width, n * pos), BF16), vm((width, n * pos), BF16),
            vm((sl, n * pos), BF16), vm((2, sl, n * pos), F32),
            vm((pieces, table, pos), F32), vm((pieces, table, pos), BF16),
            vm((pieces, table, pos), BF16),
            vm((count, nb, packed, 128), BF16), vm((count, outer, packed, 128), BF16),
            vm((count, outer - 1, packed, 128), BF16), vm((count, outer - 1, packed, 128), BF16),
            vm((2, 2, pieces, 3, half, pos), BF16), vm((2, pieces, 3, half, pos), BF16),
            vm((3, width, pos), F32),
            dma((8,)), dma((3,)), dma((3,)), dma((2, 3)), dma((2, 3)),
            dma((pieces, 3)), dma((pieces, 3)), dma((pieces, 3)), dma((pieces, 3)),
            dma((pieces, 3)), dma((pieces, 3)), dma((pieces,)), dma((pieces,)),
            dma((2, pieces)), dma((2, pieces)),
            dma((count, outer)), dma((count, outer)), dma((count, outer - 1)), dma((count, outer - 1)),
        ],
        compiler_params=pltpu.CompilerParams(
            collective_id=0, has_side_effects=True, vmem_limit_bytes=60 * 1024 * 1024
        ),
    )(
        live_counts, spatial_gate, temporal_gate,
        spatial_qkv.reshape(3, pos, width), temporal_qkv.reshape(3, pos, width),
        cotangent.reshape(pos, width), temporal_proj.reshape(n, sl, width),
    )
    grads, first, second = pl.pallas_call(
        functools.partial(finish, units),
        out_shape=(
            jax.ShapeDtypeStruct((3, pos, width), BF16),
            jax.ShapeDtypeStruct((rows, sl), F32),
            jax.ShapeDtypeStruct((rows, sl), F32),
        ),
        in_specs=[whole, whole],
        out_specs=tuple(pl.BlockSpec(memory_space=pltpu.HBM) for _ in range(3)),
        scratch_shapes=[vm((rows, sl), F32), vm((rows, sl), F32), dma((3 + 2,))],
        compiler_params=pltpu.CompilerParams(vmem_limit_bytes=4 * 1024 * 1024),
    )(grads, sums)
    return grads[None, :, None], first.T, second.T


def solution(mesh):
    n, nb = mesh.shape["seq"], mesh.shape["dp"]

    def chosen(*args):
        cot = args[2]
        _, frames, pos, width = cot.shape
        fits = frames == 1 and pos == 128 and width == HEADS * HD and n % 2 == 0 and nb % 2 == 0
        fits = fits and n == 4 and nb > 2 and HEADS % n == 0
        if fits and width // n % 16 == 0 and width // nb % 16 == 0:
            return kernel_body(n, nb, *args)
        return body(*args)

    return jax.shard_map(
        chosen,
        mesh=mesh,
        in_specs=(
            P("dp", None, "seq", None, None),
            P("dp", None, "seq", None, None),
            P("dp", "seq", None, None),
            P("dp", None),
            P("dp", None),
            P(),
            P("dp", None),
        ),
        out_specs=(P("dp", None, "seq", None, None), P("seq", "dp"), P("seq", "dp")),
        check_vma=False,
    )
```
